32 devices in a mesh: pheno: 2 (over x), samp: 8 (over z, y), var: 2 (over core).
Axes of the slice: x: 2, y: 2, z: 4, core: 2. Of those that a mesh axis runs over, the one named last changes fastest.
Arguments:
- genotypes: bfloat16 [4608, 16384], P('samp', 'var'), may hold values from -6 to 6, as said below
- coefficients: float32 [64, 16384], P('pheno', 'var'), parts along dimension 0, may hold values from -0.5 to 0.5
- time_order: int32 [9216], P(('pheno', 'samp')), parts along dimension 0, may hold values from 0 to 4607, as said below
- fold_label: int32 [9216], P(('pheno', 'samp')), parts along dimension 0, may hold values from 0 to 7
- event_flag: int32 [9216], P(('pheno', 'samp')), parts along dimension 0, may hold values 0 or 1
- penalty: float32 [32], replicated, may hold values from 0.3 to 1.5
- step_size: float32 [32], replicated, may hold values from 0.2 to 1
Outputs:
- coefficients_out: float32 [64, 16384], P('pheno', 'var'), parts along dimension 0
- score: bfloat16 [64, 4608], P('pheno', 'samp'), parts along dimension 0
The draws below stay inside these ranges and needn't reach their ends.
There are 2 independent parts, one for each index of `pheno`. The reference program is written for one: setup_inputs(seed, part) draws one part's arguments, and reference() takes and returns one part's arrays. A program takes and returns all parts, laid end to end along the dimension named above; an argument that names none is the same for every part. Nothing has to cross between parts.
Inputs may be any that keep to these rules, and one draw needn't show every extreme that they name: time_order names every sample ID once; each block of 576 consecutive IDs holds exactly 576 / 8 of the IDs in each block of 576 consecutive time ranks. `genotypes`: entries of mean zero and unit variance.
All inputs are finite; a program needn't handle non-finite values. No bound on the sum of `event_flag` on one device may be relied on, other than what follows from the above.
Results may differ from the reference program's by a relative error of at most 0.0027.
Values may be sent and summed in bfloat16 or wider, within the bound.
A program may use at most 64 MiB of HBM per device.

```python
import math
import jax
import jax.numpy as jnp
from jax import lax

S_DEV = 576
VARS = 16384
COLS = 32
FOLDS = 8
ITERS = 3
SAMPLES = 4608
N_SAMP = 8


def draw_time_order(key, part):
    share = S_DEV // N_SAMP
    first_key = jax.random.fold_in(key, 11)
    second_key = jax.random.fold_in(key, 23)
    identity = jnp.arange(SAMPLES, dtype=jnp.int32).reshape(N_SAMP, S_DEV)
    row_keys = jax.random.split(first_key, N_SAMP)
    mixed = jax.vmap(lambda one_key, row: jax.random.permutation(one_key, row))(row_keys, identity)
    grouped = mixed.reshape(N_SAMP, N_SAMP, share).transpose(1, 0, 2).reshape(N_SAMP, S_DEV)
    block_keys = jax.random.split(second_key, N_SAMP)
    ranked = jax.vmap(lambda one_key, row: jax.random.permutation(one_key, row))(block_keys, grouped)
    return ranked.reshape(SAMPLES).astype(jnp.int32)


def draw_genotypes(key, part):
    own_key = jax.random.fold_in(key, 37)
    values = jnp.clip(jax.random.normal(own_key, (SAMPLES, VARS), jnp.float32), -6.0, 6.0)
    return values.astype(jnp.bfloat16)


def with_ends(drawn, stream_key, smallest, largest):
    longest = drawn.shape.index(max(drawn.shape))
    spots = []
    for shift in (0, 1):
        where = [jax.random.randint(jax.random.fold_in(stream_key, axis), (), 0, length) for axis, length in enumerate(drawn.shape)]
        where[longest] = (where[longest] + shift) % drawn.shape[longest]
        spots.append(tuple(where))
    return drawn.at[spots[0]].set(smallest).at[spots[1]].set(largest)


def block_levels(key, extent, cuts, low, largest):
    def one(dim, parts):
        draws = jax.random.uniform(jax.random.fold_in(jax.random.fold_in(key, 6), dim), (parts,), jnp.float32, low / len(cuts), largest / len(cuts))
        return jnp.repeat(jnp.exp(draws), extent[dim] // parts).reshape((-1,) + (1,) * (len(extent) - dim - 1))

    gain = one(*cuts[0])
    for cut in cuts[1:]:
        gain = gain * one(*cut)
    return gain


def setup_inputs(seed: int = 0, part: int = 0) -> dict:
    seeds = jax.random.split(jax.random.key(seed), 8)
    own_keys = jax.random.split(jax.random.fold_in(seeds[7], part), 8)
    return {
        "genotypes": draw_genotypes(jax.random.fold_in(seeds[7], 71), part),
        "coefficients": jnp.clip(jax.random.uniform(own_keys[1], (COLS, VARS), jnp.float32, -0.5, 0.5) * block_levels(own_keys[1], (COLS, VARS), ((1, 2),), -0.4, 0.0), -0.5, 0.5),
        "time_order": draw_time_order(jax.random.fold_in(jax.random.fold_in(seeds[7], part), 71), part),
        "fold_label": with_ends(jax.random.randint(own_keys[3], (SAMPLES,), 0, FOLDS), jax.random.fold_in(own_keys[3], 1), 0, FOLDS - 1).astype(jnp.int32),
        "event_flag": with_ends((jax.random.randint(own_keys[4], (SAMPLES,), 0, 3) < 1).astype(jnp.int32), jax.random.fold_in(own_keys[4], 1), 0, 1),
        "penalty": jnp.clip(jnp.exp(jax.random.uniform(seeds[5], (COLS,), jnp.float32, math.log(0.3), math.log(1.5))), 0.3, 1.5),
        "step_size": jnp.clip(jnp.exp(jax.random.uniform(seeds[6], (COLS,), jnp.float32, math.log(0.2), math.log(1.0))), 0.2, 1.0),
    }


def shrink(coef, gradient, penalty, step_size):
    stepped = coef - step_size[:, None] * gradient
    threshold = (step_size * penalty)[:, None]
    return jnp.sign(stepped) * jnp.maximum(jnp.abs(stepped) - threshold, 0.0)

def reference(genotypes, coefficients, time_order, fold_label, event_flag, penalty, step_size):
    column_fold = jnp.arange(COLS, dtype=jnp.int32) % FOLDS
    fold_time = fold_label[time_order]
    event_time = event_flag[time_order].astype(jnp.float32)
    train_mask = (fold_time[None, :] != column_fold[:, None]).astype(jnp.float32)
    events_kept = train_mask * event_time[None, :]
    coef = coefficients
    score_low = jnp.zeros((COLS, SAMPLES), jnp.bfloat16)
    for step in range(ITERS):
        coef_low = coef.astype(jnp.bfloat16)
        predictor = lax.dot_general(coef_low, genotypes, (((1,), (1,)), ((), ())), preferred_element_type=jnp.float32)
        predictor = predictor * (1.0 / math.sqrt(VARS))
        weight = train_mask * jnp.exp(predictor[:, time_order])
        risk = lax.cumsum(weight, axis=1, reverse=True)
        ratio = events_kept / jnp.where(events_kept > 0, risk, 1.0)
        hazard = lax.cumsum(ratio, axis=1)
        score_time = (weight * hazard - events_kept).astype(jnp.bfloat16)
        score_low = jnp.zeros((COLS, SAMPLES), jnp.bfloat16).at[:, time_order].set(score_time)
        gradient = jnp.dot(score_low, genotypes, preferred_element_type=jnp.float32) * (1.0 / math.sqrt(SAMPLES))
        coef = shrink(coef, gradient, penalty, step_size)
    return (coef, score_low)
```

```python
import functools
import math

import jax
import jax.numpy as jnp
from jax import lax
from jax.experimental import pallas as pl
from jax.experimental.pallas import tpu as pltpu
from jax.sharding import PartitionSpec as P

VARS = 16384
FOLDS = 8
ITERS = 3
MESH = pl.DeviceIdType.MESH
CUTS_LOW = 1
CUTS_SUM = 2
CUTS_LAST = 2
F32 = jnp.float32
BF16 = jnp.bfloat16


def each(count, body):
    if count <= 8:
        for step in range(count):
            body(step)
    else:
        lax.fori_loop(0, count, lambda step, carry: (body(step), carry)[1], 0)


def halves(value):
    high = value.astype(BF16)
    low = (value - high.astype(F32)).astype(BF16)
    return jnp.concatenate([high, low], axis=0)


def across(left, right):
    return lax.dot_general(left, right, (((1,), (1,)), ((), ())), preferred_element_type=F32)


def across2(value, matrix):
    rows = value.shape[0]
    both = across(halves(value), matrix)
    return both[:rows] + both[rows:]


def dot2(value, matrix):
    rows = value.shape[0]
    both = jnp.dot(halves(value), matrix, preferred_element_type=F32)
    return both[:rows] + both[rows:]


def path_kernel(
    count, scale_vars, scale_samples,
    geno_in, coef_in, codes, step_row, penalty_row,
    low_out, change_out, score_out,
    geno, coef, to_time, later, earlier, to_id, mask, kept, kept_time, place_out, place_in, spot, code_out, code_in,
    low, change, shard, half_send, half_recv, out_a, in_a, out_b, in_b,
    out_y, in_y, out_z, in_z, own_g, pred, held, score, score_wide,
    geno_sem, coef_sem, end_sem, change_sem, s_ss, s_rs, half_ss, half_rs, p_ss, p_rs, l_ss, l_rs, a_ss, a_rs, b_ss, b_rs,
    y_ss, y_rs, z_ss, z_rs, c_ss, c_rs, fwd_ss, fwd_rs, f_ss, f_rs, last_ss, last_rs,
):
    me = lax.axis_index("samp")
    var = lax.axis_index("var")
    columns, variants = coef.shape
    rows = geno.shape[0]
    part = variants // count
    width = later.shape[1] // count
    share = rows // count
    half = count // 2
    few = columns // 2
    mine = pl.ds(pl.multiple_of(var * few, few), few)
    theirs = pl.ds(pl.multiple_of((1 - var) * few, few), few)
    side = 1 - 2 * lax.rem(me, 2)

    def peer(step):
        return lax.rem(me + step, count)

    def down(hop):
        return lax.rem(me + 2 * hop, count)

    def up(hop):
        return lax.rem(me + count - 2 * hop, count)

    def piece(owner):
        return pl.ds(pl.multiple_of(owner * part, part), part)

    def band(number, cuts):
        cut = columns // cuts
        return pl.ds(number * cut, cut)

    def hops(body):
        if half <= 8:
            for hop in sorted(range(1, half), key=lambda hop: (abs(2 * hop - half), hop)):
                body(hop)
        else:
            lax.fori_loop(1, half, lambda hop, carry: (body(hop), carry)[1], 0)

    def slots(owner):
        return pl.ds(pl.multiple_of(owner * width, width), width)

    def block_load(owner):
        return pltpu.make_async_copy(geno_in.at[:, piece(owner)], geno.at[:, piece(owner)], geno_sem.at[owner])

    coef_load = pltpu.make_async_copy(coef_in, coef, coef_sem)
    coef_load.start()
    each(count, lambda owner: block_load(owner).start())

    barrier = pltpu.get_barrier_semaphore()

    def greet(step):
        pl.semaphore_signal(barrier, inc=1, device_id={"samp": peer(step + 1)}, device_id_type=MESH)

    each(count - 1, greet)
    pl.semaphore_signal(barrier, inc=1, device_id={"var": 1 - var}, device_id_type=MESH)

    def remote(source, target, ssem, rsem, owner):
        return pltpu.make_async_remote_copy(
            src_ref=source, dst_ref=target, send_sem=ssem, recv_sem=rsem,
            device_id={"samp": owner}, device_id_type=MESH,
        )

    def send(source, target, ssem, rsem, owner):
        return remote(source, target, ssem.at[owner], rsem.at[me], owner)

    def arrive(source, target, ssem, rsem, owner):
        remote(source, target, ssem.at[owner], rsem.at[owner], owner).wait_recv()

    def swap_with(source, target, ssem, rsem):
        return pltpu.make_async_remote_copy(
            src_ref=source, dst_ref=target, send_sem=ssem, recv_sem=rsem,
            device_id={"var": 1 - var}, device_id_type=MESH,
        )

    ids_row = codes[0:1, :].astype(F32)
    down_ranks = lax.broadcasted_iota(jnp.int32, (rows, rows), 0)
    along_ranks = lax.broadcasted_iota(jnp.int32, (rows, rows), 1)
    ids = jnp.sum(jnp.where(down_ranks == along_ranks, ids_row, 0.0), axis=1, keepdims=True)
    owner_row = jnp.zeros_like(ids_row)
    owner_of = jnp.zeros_like(ids)
    for owner in range(1, count):
        owner_row += jnp.where(ids_row >= owner * rows, 1.0, 0.0)
        owner_of += jnp.where(ids >= owner * rows, 1.0, 0.0)
    before = jnp.sum(
        jnp.where((owner_row == owner_of) & (along_ranks < down_ranks), 1.0, 0.0), axis=1, keepdims=True
    )
    key = (owner_of * width + before).astype(jnp.int32)
    place = (ids - owner_of * rows).astype(jnp.int32)
    ranks = lax.broadcasted_iota(jnp.int32, (rows, width), 0)
    lane = lax.broadcasted_iota(jnp.int32, (rows, width), 1)
    for owner in range(count):
        match = key == lane + owner * width
        place_out[owner] = jnp.max(jnp.where(match, place, -1), axis=0, keepdims=True)
        spot[owner] = jnp.max(jnp.where(match, ranks, -1), axis=0, keepdims=True)

    line = lax.broadcasted_iota(jnp.int32, (8, rows), 0)
    code = codes[1:2, :]
    labels = jnp.where(line == 0, code // 2, jnp.where(line == 1, code % 2, 0)).astype(F32)
    same = lax.broadcasted_iota(jnp.int32, (columns, columns), 0) == lax.broadcasted_iota(
        jnp.int32, (columns, columns), 1
    )
    pace = jnp.sum(jnp.where(same, step_row[...], 0.0), axis=1, keepdims=True)
    threshold = pace * jnp.sum(jnp.where(same, penalty_row[...], 0.0), axis=1, keepdims=True)
    column_fold = lax.rem(lax.broadcasted_iota(jnp.int32, (few, rows), 0) + var * few, FOLDS).astype(F32)
    mask[...] = jnp.where(labels[0:1, :] != column_fold, 1.0, 0.0)
    kept[...] = mask[...] * labels[1:2, :]
    place_in[me] = place_out[me]

    pl.semaphore_wait(barrier, count)

    def push_p(step):
        owner = peer(step + 1)
        send(place_out.at[owner], place_in.at[me], p_ss, p_rs, owner).start()
    each(count - 1, push_p)

    coef_load.wait()
    low[...] = coef[...].astype(BF16)
    shard[...] = coef[:, piece(me)]

    def arrange():
        block = jnp.zeros((rows, width), jnp.int32)

        def land_p(step):
            owner = peer(step + 1)
            arrive(place_out.at[owner], place_in.at[owner], p_ss, p_rs, owner)
            send(place_out.at[owner], place_in.at[me], p_ss, p_rs, owner).wait_send()
        each(count - 1, land_p)
        for owner in range(1, count):
            block += jnp.where(place_in[owner] == ranks, owner, 0)
        block = jnp.broadcast_to(jnp.sum(block, axis=1, keepdims=True), (rows, width))
        in_totals = (lane - share) == block
        for owner in range(count):
            span = slice(owner * width, (owner + 1) * width)
            hit = place_in[owner] == ranks
            to_time[:, span] = jnp.where(hit | in_totals, 1.0, 0.0).astype(BF16)
            to_id[:, span] = jnp.where(hit | ((lane == share) & (block > owner)), 1.0, 0.0).astype(BF16)
        spread = jnp.dot(labels.astype(BF16), to_time[...], preferred_element_type=F32)
        for owner in range(count):
            code_out[owner] = spread[:, owner * width:(owner + 1) * width]

        def push_l(step):
            owner = peer(step + 1)
            send(code_out.at[owner], code_in.at[me], l_ss, l_rs, owner).start()
        each(count - 1, push_l)
        code_in[me] = code_out[me]

    def sums():
        place_line = lax.broadcasted_iota(jnp.int32, (1, width), 1)
        for owner in range(count):
            span = slice(owner * width, (owner + 1) * width)
            beyond = (place_line >= share + me + 1) & (place_line < share + count)
            reach = jnp.where(beyond, rows, spot[owner])
            back = jnp.where(place_line == share, rows, spot[owner])
            later[:, span] = jnp.where(reach >= ranks, 1.0, 0.0).astype(BF16)
            earlier[:, span] = jnp.where(back >= ranks, 1.0, 0.0).astype(BF16)

    def time_labels():
        def land_l(step):
            owner = peer(step + 1)
            arrive(code_out.at[owner], code_in.at[owner], l_ss, l_rs, owner)
            send(code_out.at[owner], code_in.at[me], l_ss, l_rs, owner).wait_send()
        each(count - 1, land_l)
        labels_time = jnp.zeros((labels.shape[0], rows), F32)
        for owner in range(count):
            labels_time += across(
                code_in[owner].astype(BF16), jnp.where(spot[owner] == ranks, 1.0, 0.0).astype(BF16)
            )
        kept_time[...] = jnp.where(labels_time[0:1, :] != column_fold, 1.0, 0.0) * labels_time[1:2, :]

    def low_out_of(hop, number):
        part_of = low.at[band(number, CUTS_LOW), piece(me)]
        owner = me + side if hop is None else down(hop)
        index = (0 if hop is None else hop, number)
        return remote(part_of, part_of, c_ss.at[index], c_rs.at[index], owner)

    def low_relay(hop, number):
        part_of = low.at[band(number, CUTS_LOW), piece(up(hop))]
        return remote(part_of, part_of, fwd_ss.at[hop, number], fwd_rs.at[hop, number], me + side)

    def change_own(hop, number):
        index = (0 if hop is None else hop, number)
        bands = band(number, CUTS_LAST)
        source = change.at[bands, piece(me)]
        target = change_out.at[bands, piece(me)] if hop is None else source
        owner = me + side if hop is None else down(hop)
        return remote(source, target, f_ss.at[index], f_rs.at[index], owner)

    def change_relay(hop, number):
        bands = band(number, CUTS_LAST)
        return remote(
            change.at[bands, piece(up(hop))], change_out.at[bands, piece(up(hop))],
            last_ss.at[hop, number], last_rs.at[hop, number], me + side,
        )

    def change_keep(hop):
        owner = up(hop)
        return pltpu.make_async_copy(change.at[:, piece(owner)], change_out.at[:, piece(owner)], change_sem.at[hop])

    def send_y(hop, number):
        bands = band(number, CUTS_SUM)
        return remote(
            out_y.at[hop, bands, :], in_y.at[hop, bands, :], y_ss.at[hop, number], y_rs.at[hop, number], me + side
        )

    def send_z(hop, number):
        bands = band(number, CUTS_SUM)
        return remote(
            out_z.at[hop, bands, :], in_z.at[hop, bands, :], z_ss.at[hop, number], z_rs.at[hop, number], down(hop)
        )

    def add_part(owner):
        pred[...] += across(low[:, piece(owner)], geno[:, piece(owner)])

    def one_step(turn, first):
        if first:
            pred[...] = jnp.zeros_like(pred)

            def add_block(owner):
                block_load(owner).wait()
                add_part(owner)
            each(count, add_block)
        else:
            pred[...] = across(low[:, piece(me)], geno[:, piece(me)])
            for number in range(CUTS_LOW):
                low_out_of(None, number).wait_recv()
            add_part(me + side)

            def pass_on(hop):
                for number in range(CUTS_LOW):
                    low_out_of(hop, number).wait_recv()
                    low_relay(hop, number).start()
            hops(pass_on)
            hops(lambda hop: add_part(up(hop)))

            def add_side(hop):
                for number in range(CUTS_LOW):
                    low_relay(hop, number).wait_recv()
                add_part(up(hop) + side)
            hops(add_side)

        half_send[...] = pred[theirs, :]
        slot = lax.rem(turn, 2)
        swap = swap_with(half_send, half_recv.at[slot], half_ss, half_rs.at[slot])
        swap.start()
        if first:
            arrange()
        else:
            for number in range(CUTS_LOW):
                low_out_of(None, number).wait_send()

                def low_done(hop):
                    low_out_of(hop, number).wait_send()
                    low_relay(hop, number).wait_send()
                hops(low_done)
        swap.wait()

        weight = mask[...] * jnp.exp((pred[mine, :] + half_recv[slot]) * scale_vars)
        held[...] = weight
        spread = dot2(weight, to_time[...])
        for owner in range(count):
            out_a[owner] = spread[:, owner * width:(owner + 1) * width]

        def push_a(step):
            owner = peer(step + 1)
            send(out_a.at[owner], in_a.at[me], a_ss, a_rs, owner).start()
        each(count - 1, push_a)
        if first:
            sums()
            time_labels()
        risk = across2(out_a[me], later[:, slots(me)])
        for step in range(count - 1):
            owner = peer(step + 1)
            arrive(out_a.at[owner], in_a.at[owner], a_ss, a_rs, owner)
            risk += across2(in_a[owner], later[:, slots(owner)])
        events = kept_time[...]
        ratio = events / jnp.where(events > 0, risk, 1.0)
        spread = dot2(ratio, earlier[...])
        for owner in range(count):
            out_b[owner] = spread[:, owner * width:(owner + 1) * width]

        def push_b(step):
            owner = peer(step + 1)
            send(out_b.at[owner], in_b.at[me], b_ss, b_rs, owner).start()
        each(count - 1, push_b)
        hazard = across2(out_b[me], to_id[:, slots(me)])
        for step in range(count - 1):
            owner = peer(step + 1)
            arrive(out_b.at[owner], in_b.at[owner], b_ss, b_rs, owner)
            hazard += across2(in_b[owner], to_id[:, slots(owner)])
        score[mine, :] = (held[...] * hazard - kept[...]).astype(BF16)
        trade = swap_with(score.at[mine, :], score.at[mine, :], s_ss, s_rs)
        trade.start()
        trade.wait()

        def product(owner):
            return jnp.dot(score[...], geno[:, piece(owner)], preferred_element_type=F32)

        def give(hop):
            out_y[hop] = product(down(hop) + side).astype(BF16)
            for number in range(CUTS_SUM):
                send_y(hop, number).start()

        def keep(hop):
            own_g[hop] = product(down(hop))

        hops(give)
        give(0)
        hops(keep)
        keep(0)

        def gather_pair(hop):
            for number in range(CUTS_SUM):
                bands = band(number, CUTS_SUM)
                send_y(hop, number).wait_recv()
                out_z[hop, bands, :] = (own_g[hop, bands, :] + in_y[hop, bands, :].astype(F32)).astype(BF16)
                send_z(hop, number).start()
        hops(gather_pair)
        for number in range(CUTS_SUM):
            send_y(0, number).wait_recv()
        shard_sum = own_g.at[0]
        shard_sum[...] += in_y[0].astype(F32)

        def gather_all(hop):
            for number in range(CUTS_SUM):
                send_z(hop, number).wait_recv()
            shard_sum[...] += in_z[hop].astype(F32)
        hops(gather_all)
        stepped = shard[...] - pace * (shard_sum[...] * scale_samples)
        shrunk = jnp.maximum(jnp.abs(stepped) - threshold, 0.0)
        fresh = jnp.where(stepped > 0, shrunk, -shrunk)
        shard[...] = fresh

        def spread_low():
            low[:, piece(me)] = fresh.astype(BF16)
            for number in range(CUTS_LOW):
                hops(lambda hop: low_out_of(hop, number).start())
                low_out_of(None, number).start()

        if first:
            spread_low()
        else:
            pl.when(turn < ITERS - 1)(spread_low)

        def drained(step):
            owner = peer(step + 1)
            send(out_a.at[owner], in_a.at[me], a_ss, a_rs, owner).wait_send()
            send(out_b.at[owner], in_b.at[me], b_ss, b_rs, owner).wait_send()
        each(count - 1, drained)

        def sent(hop):
            for number in range(CUTS_SUM):
                send_y(hop, number).wait_send()
                send_z(hop, number).wait_send()
        hops(sent)
        for number in range(CUTS_SUM):
            send_y(0, number).wait_send()

    one_step(0, True)
    lax.fori_loop(1, ITERS, lambda turn, carry: (one_step(turn, False), carry)[1], 0)

    change[:, piece(me)] = (shard[...] - low[:, piece(me)].astype(F32)).astype(BF16)
    for number in range(CUTS_LAST):
        hops(lambda hop: change_own(hop, number).start())
        change_own(None, number).start()
    own_keep = change_keep(0)
    own_keep.start()
    low_keep = pltpu.make_async_copy(low, low_out, end_sem.at[0])
    low_keep.start()
    score_wide[...] = score[...].astype(F32)
    score_keep = pltpu.make_async_copy(score_wide, score_out, end_sem.at[1])
    score_keep.start()

    def pass_change(number):
        def go(hop):
            change_own(hop, number).wait_recv()
            change_relay(hop, number).start()
            if number == CUTS_LAST - 1:
                change_keep(hop).start()
        hops(go)
    for number in range(CUTS_LAST):
        pass_change(number)
    own_keep.wait()
    low_keep.wait()
    score_keep.wait()

    def finish(hop):
        change_keep(hop).wait()
        for number in range(CUTS_LAST):
            change_own(hop, number).wait_send()
            change_relay(hop, number).wait()
    hops(finish)
    for number in range(CUTS_LAST):
        change_own(None, number).wait()


def local(genotypes, coefficients, time_order, fold_label, event_flag, penalty, step_size):
    rows = genotypes.shape[0]
    columns, variants = coefficients.shape
    count = lax.axis_size("samp")
    half = count // 2
    share = rows // count
    width = -(-(share + count) // 128) * 128
    total = count * width
    part = variants // count
    few = columns // 2

    codes = jnp.stack([time_order, fold_label * 2 + event_flag])
    vmem = pl.BlockSpec(memory_space=pltpu.VMEM)
    away = pl.BlockSpec(memory_space=pl.ANY)
    dma = pltpu.SemaphoreType.DMA
    low, change, score = pl.pallas_call(
        functools.partial(path_kernel, count, 1.0 / math.sqrt(VARS), 1.0 / math.sqrt(rows * count)),
        out_shape=(
            jax.ShapeDtypeStruct((columns, variants), BF16),
            jax.ShapeDtypeStruct((columns, variants), BF16),
            jax.ShapeDtypeStruct((columns, rows), F32),
        ),
        in_specs=[away] * 2 + [vmem] * 3,
        out_specs=(away, away, away),
        scratch_shapes=[
            pltpu.VMEM((rows, variants), BF16),
            pltpu.VMEM((columns, variants), F32),
            pltpu.VMEM((rows, total), BF16),
            pltpu.VMEM((rows, total), BF16),
            pltpu.VMEM((rows, total), BF16),
            pltpu.VMEM((rows, total), BF16),
            pltpu.VMEM((few, rows), F32),
            pltpu.VMEM((few, rows), F32),
            pltpu.VMEM((few, rows), F32),
            pltpu.VMEM((count, 1, width), jnp.int32),
            pltpu.VMEM((count, 1, width), jnp.int32),
            pltpu.VMEM((count, 1, width), jnp.int32),
            pltpu.VMEM((count, 8, width), F32),
            pltpu.VMEM((count, 8, width), F32),
            pltpu.VMEM((columns, variants), BF16),
            pltpu.VMEM((columns, variants), BF16),
            pltpu.VMEM((columns, part), F32),
            pltpu.VMEM((few, rows), F32),
            pltpu.VMEM((2, few, rows), F32),
            pltpu.VMEM((count, few, width), F32),
            pltpu.VMEM((count, few, width), F32),
            pltpu.VMEM((count, few, width), F32),
            pltpu.VMEM((count, few, width), F32),
            pltpu.VMEM((half, columns, part), BF16),
            pltpu.VMEM((half, columns, part), BF16),
            pltpu.VMEM((half, columns, part), BF16),
            pltpu.VMEM((half, columns, part), BF16),
            pltpu.VMEM((half, columns, part), F32),
            pltpu.VMEM((columns, rows), F32),
            pltpu.VMEM((few, rows), F32),
            pltpu.VMEM((columns, rows), BF16),
            pltpu.VMEM((columns, rows), F32),
            dma((count,)), dma, dma((2,)), dma((half,)),
            dma, dma, dma, dma((2,)),
        ] + [dma((count,))] * 8 + [dma((half, CUTS_SUM))] * 4 + [dma((half, CUTS_LOW))] * 4
        + [dma((half, CUTS_LAST))] * 4,
        compiler_params=pltpu.CompilerParams(
            collective_id=0, has_side_effects=True, vmem_limit_bytes=48 * 1024 * 1024
        ),
    )(genotypes, coefficients, codes, step_size[None], penalty[None])
    return low.astype(F32) + change.astype(F32), score.astype(BF16)


def solution(mesh):
    placed = (
        P("samp", "var"),
        P("pheno", "var"),
        P(("pheno", "samp")),
        P(("pheno", "samp")),
        P(("pheno", "samp")),
        P(),
        P(),
    )
    return jax.shard_map(
        local,
        mesh=mesh,
        in_specs=placed,
        out_specs=(P("pheno", "var"), P("pheno", "samp")),
        check_vma=False,
    )
```

```python
import functools
import math

import jax
import jax.numpy as jnp
from jax import lax
from jax.experimental import pallas as pl
from jax.experimental.pallas import tpu as pltpu
from jax.sharding import PartitionSpec as P

VARS = 16384
FOLDS = 8
ITERS = 3
MESH = pl.DeviceIdType.MESH
F32 = jnp.float32
BF16 = jnp.bfloat16


def each(count, body):
    if count <= 8:
        for step in range(count):
            body(step)
    else:
        lax.fori_loop(0, count, lambda step, carry: (body(step), carry)[1], 0)


def halves(value):
    high = value.astype(BF16)
    low = (value - high.astype(F32)).astype(BF16)
    return jnp.concatenate([high, low], axis=0)


def across(left, right):
    return lax.dot_general(left, right, (((1,), (1,)), ((), ())), preferred_element_type=F32)


def across2(value, matrix):
    rows = value.shape[0]
    both = across(halves(value), matrix)
    return both[:rows] + both[rows:]


def dot2(value, matrix):
    rows = value.shape[0]
    both = jnp.dot(halves(value), matrix, preferred_element_type=F32)
    return both[:rows] + both[rows:]


def path_kernel(
    count, scale_vars, scale_samples,
    geno_in, coef_in, facts,
    low_out, change_out, score_out,
    geno, coef, to_time, later, earlier, to_id, mask, kept, kept_time, place_out, place_in, spot, code_out, code_in,
    low, change, shard, pace, threshold, half_recv, out_a, in_a, out_b, in_b,
    out_y, in_y, out_z, in_z, own_g, pred, held, score, score_wide,
    geno_sem, coef_sem, end_sem, keep_sem, s_ss, s_rs, half_ss, half_rs, p_ss, l_ss, a_ss, b_ss, y_ss, z_ss,
    p_rs, l_rs, a_rs, b_rs, y_rs, z_rs, c_ss, c_rs, fwd_ss, fwd_rs,
):
    me = lax.axis_index("samp")
    var = lax.axis_index("var")
    columns, variants = coef.shape
    rows = geno.shape[0]
    part = variants // count
    width = later.shape[1] // count
    share = rows // count
    half = count // 2
    few = columns // 2
    side = 1 - 2 * lax.rem(me, 2)

    def peer(step):
        return lax.rem(me + step, count)

    def down(hop):
        return lax.rem(me + 2 * hop, count)

    def up(hop):
        return lax.rem(me + count - 2 * hop, count)

    def piece(owner):
        return pl.ds(pl.multiple_of(owner * part, part), part)

    def hops(body):
        if half <= 8:
            for hop in sorted(range(1, half), key=lambda hop: (abs(2 * hop - half), hop)):
                body(hop)
        else:
            lax.fori_loop(1, half, lambda hop, carry: (body(hop), carry)[1], 0)

    def slots(owner):
        return pl.ds(pl.multiple_of(owner * width, width), width)

    def block_load(owner):
        return pltpu.make_async_copy(geno_in.at[:, piece(owner)], geno.at[:, piece(owner)], geno_sem.at[owner])

    coef_load = pltpu.make_async_copy(coef_in, coef, coef_sem)
    coef_load.start()
    each(count, lambda owner: block_load(owner).start())

    barrier = pltpu.get_barrier_semaphore()

    def greet(step):
        pl.semaphore_signal(barrier, inc=1, device_id={"samp": peer(step + 1)}, device_id_type=MESH)

    each(count - 1, greet)
    pl.semaphore_signal(barrier, inc=1, device_id={"var": 1 - var}, device_id_type=MESH)

    def remote(source, target, ssem, rsem, owner):
        return pltpu.make_async_remote_copy(
            src_ref=source, dst_ref=target, send_sem=ssem, recv_sem=rsem,
            device_id={"samp": owner}, device_id_type=MESH,
        )

    def scatter(source, target, ssem, rsem):
        def push(step):
            owner = peer(step + 1)
            remote(source.at[owner], target.at[me], ssem, rsem.at[me], owner).start()
        each(count - 1, push)

    def arrive(target, rsem, owner):
        remote(target.at[owner], target.at[owner], rsem.at[owner], rsem.at[owner], owner).wait_recv()

    def scattered(source, ssem):
        most = source.at[pl.ds(0, count - 1)]
        remote(most, most, ssem, ssem, me + side).wait_send()

    def swap_with(source, target, ssem, rsem):
        return pltpu.make_async_remote_copy(
            src_ref=source, dst_ref=target, send_sem=ssem, recv_sem=rsem,
            device_id={"var": 1 - var}, device_id_type=MESH,
        )

    ids_row = facts[0:1, :]
    down_ranks = lax.broadcasted_iota(jnp.int32, (rows, rows), 0)
    along_ranks = lax.broadcasted_iota(jnp.int32, (rows, rows), 1)
    ids = jnp.sum(jnp.where(down_ranks == along_ranks, ids_row, 0.0), axis=1, keepdims=True)
    owner_row = jnp.zeros_like(ids_row)
    owner_of = jnp.zeros_like(ids)
    for owner in range(1, count):
        owner_row += jnp.where(ids_row >= owner * rows, 1.0, 0.0)
        owner_of += jnp.where(ids >= owner * rows, 1.0, 0.0)
    before = jnp.sum(
        jnp.where((owner_row == owner_of) & (along_ranks < down_ranks), 1.0, 0.0), axis=1, keepdims=True
    )
    key = (owner_of * width + before).astype(jnp.int32)
    place = (ids - owner_of * rows).astype(jnp.int32)
    ranks = lax.broadcasted_iota(jnp.int32, (rows, width), 0)
    lane = lax.broadcasted_iota(jnp.int32, (rows, width), 1)
    for owner in range(count):
        match = key == lane + owner * width
        place_out[owner] = jnp.max(jnp.where(match, place, -1), axis=0, keepdims=True)
        spot[owner] = jnp.max(jnp.where(match, ranks, -1), axis=0, keepdims=True)

    line = lax.broadcasted_iota(jnp.int32, (8, rows), 0)
    labels = jnp.where(line == 0, facts[1:2, :], jnp.where(line == 1, facts[2:3, :], 0.0))
    same = lax.broadcasted_iota(jnp.int32, (columns, columns), 0) == lax.broadcasted_iota(
        jnp.int32, (columns, columns), 1
    )
    step_size = jnp.sum(jnp.where(same, facts[3:4, :columns], 0.0), axis=1, keepdims=True)
    least = step_size * jnp.sum(jnp.where(same, facts[4:5, :columns], 0.0), axis=1, keepdims=True)
    column_fold = lax.rem(lax.broadcasted_iota(jnp.int32, (columns, rows), 0), FOLDS).astype(F32)
    trained = jnp.where(labels[0:1, :] != column_fold, 1.0, 0.0)
    counted = trained * labels[1:2, :]
    for group in range(2):
        span = slice(group * few, (group + 1) * few)
        pace[group] = step_size[span]
        threshold[group] = least[span]
        mask[group] = trained[span]
        kept[group] = counted[span]
    place_in[me] = place_out[me]

    pl.semaphore_wait(barrier, count)
    scatter(place_out, place_in, p_ss, p_rs)

    coef_load.wait()
    for group in range(2):
        low[group] = coef[group * few:(group + 1) * few, :].astype(BF16)
        shard[group] = coef[group * few:(group + 1) * few, piece(me)]

    def arrange():
        block = jnp.zeros((rows, width), jnp.int32)
        each(count - 1, lambda step: arrive(place_in, p_rs, peer(step + 1)))
        scattered(place_out, p_ss)
        for owner in range(1, count):
            block += jnp.where(place_in[owner] == ranks, owner, 0)
        block = jnp.broadcast_to(jnp.sum(block, axis=1, keepdims=True), (rows, width))
        in_totals = (lane - share) == block
        for owner in range(count):
            span = slice(owner * width, (owner + 1) * width)
            hit = place_in[owner] == ranks
            to_time[:, span] = jnp.where(hit | in_totals, 1.0, 0.0).astype(BF16)
            to_id[:, span] = jnp.where(hit | ((lane == share) & (block > owner)), 1.0, 0.0).astype(BF16)
        spread = jnp.dot(labels.astype(BF16), to_time[...], preferred_element_type=F32)
        for owner in range(count):
            code_out[owner] = spread[:, owner * width:(owner + 1) * width]
        scatter(code_out, code_in, l_ss, l_rs)
        code_in[me] = code_out[me]

    def sums():
        place_line = lax.broadcasted_iota(jnp.int32, (1, width), 1)
        for owner in range(count):
            span = slice(owner * width, (owner + 1) * width)
            beyond = (place_line >= share + me + 1) & (place_line < share + count)
            reach = jnp.where(beyond, rows, spot[owner])
            back = jnp.where(place_line == share, rows, spot[owner])
            later[:, span] = jnp.where(reach >= ranks, 1.0, 0.0).astype(BF16)
            earlier[:, span] = jnp.where(back >= ranks, 1.0, 0.0).astype(BF16)

    def time_labels():
        each(count - 1, lambda step: arrive(code_in, l_rs, peer(step + 1)))
        scattered(code_out, l_ss)
        labels_time = jnp.zeros((labels.shape[0], rows), F32)
        for owner in range(count):
            labels_time += across(
                code_in[owner].astype(BF16), jnp.where(spot[owner] == ranks, 1.0, 0.0).astype(BF16)
            )
        counted_time = jnp.where(labels_time[0:1, :] != column_fold, 1.0, 0.0) * labels_time[1:2, :]
        for group in range(2):
            kept_time[group] = counted_time[group * few:(group + 1) * few]

    def tell(held_in, hop, band, group):
        block = held_in.at[group, :, piece(me)]
        owner = me + side if hop is None else down(hop)
        index = (0 if hop is None else hop, band)
        return remote(block, block, c_ss.at[index], c_rs.at[index], owner)

    def relay(held_in, end, hop, band, group):
        span = piece(up(hop))
        return remote(
            held_in.at[group, :, span], end.at[group, :, span], fwd_ss.at[hop, band], fwd_rs.at[hop, band], me + side
        )

    def tell_all(held_in, band, group):
        hops(lambda hop: tell(held_in, hop, band, group).start())
        tell(held_in, None, band, group).start()

    def pass_on(held_in, end, band, group):
        def go(hop):
            tell(held_in, hop, band, group).wait_recv()
            relay(held_in, end, hop, band, group).start()
        hops(go)

    def told(held_in, end, band, group):
        def go(hop):
            tell(held_in, hop, band, group).wait_send()
            relay(held_in, end, hop, band, group).wait_send()
        hops(go)
        tell(held_in, None, band, group).wait_send()

    def send_y(hop, band):
        return remote(out_y.at[hop, band], in_y.at[hop, band], y_ss, y_rs.at[hop, band], me + side)

    def send_z(hop, band):
        return remote(out_z.at[hop, band], in_z.at[hop, band], z_ss, z_rs.at[hop, band], down(hop))

    def add_part(owner, group):
        pred[group] += across(low[group, :, piece(owner)], geno[:, piece(owner)])

    def one_step(turn, first):
        own = lax.rem(var + turn, 2)
        other = 1 - own
        slot = lax.rem(turn, 2)
        swap = swap_with(pred.at[other], half_recv.at[slot], half_ss, half_rs.at[slot])
        if first:
            pred[...] = jnp.zeros_like(pred)

            def add_block(owner):
                block_load(owner).wait()
                both = across(low[:, :, piece(owner)].reshape(columns, part), geno[:, piece(owner)])
                pred[...] += both.reshape(2, few, rows)
            each(count, add_block)
            swap.start()
            arrange()
        else:
            def begin(band, group):
                pred[group] = across(low[group, :, piece(me)], geno[:, piece(me)])
                tell(low, None, band, group).wait_recv()
                add_part(me + side, group)

            def add_side(band, group):
                def go(hop):
                    relay(low, low, hop, band, group).wait_recv()
                    add_part(up(hop) + side, group)
                hops(go)

            begin(0, other)
            pass_on(low, low, 0, other)
            begin(1, own)
            hops(lambda hop: add_part(up(hop), other))
            pass_on(low, low, 1, own)
            add_side(0, other)
            swap.start()
            hops(lambda hop: add_part(up(hop), own))
            add_side(1, own)
            told(low, low, 0, other)
            told(low, low, 1, own)
        swap.wait()

        weight = mask[own] * jnp.exp((pred[own] + half_recv[slot]) * scale_vars)
        held[...] = weight
        spread = dot2(weight, to_time[...])
        for owner in range(count):
            out_a[owner] = spread[:, owner * width:(owner + 1) * width]
        scatter(out_a, in_a, a_ss, a_rs)
        if first:
            sums()
            time_labels()
        risk = across2(out_a[me], later[:, slots(me)])
        for step in range(count - 1):
            owner = peer(step + 1)
            arrive(in_a, a_rs, owner)
            risk += across2(in_a[owner], later[:, slots(owner)])
        events = kept_time[own]
        ratio = events / jnp.where(events > 0, risk, 1.0)
        spread = dot2(ratio, earlier[...])
        for owner in range(count):
            out_b[owner] = spread[:, owner * width:(owner + 1) * width]
        scatter(out_b, in_b, b_ss, b_rs)
        hazard = across2(out_b[me], to_id[:, slots(me)])
        for step in range(count - 1):
            owner = peer(step + 1)
            arrive(in_b, b_rs, owner)
            hazard += across2(in_b[owner], to_id[:, slots(owner)])
        score[own] = (held[...] * hazard - kept[own]).astype(BF16)
        trade = swap_with(score.at[own], score.at[own], s_ss, s_rs)
        trade.start()

        def product(left, owner):
            return jnp.dot(left, geno[:, piece(owner)], preferred_element_type=F32)

        def give(band, group):
            def go(hop):
                out_y[hop, band] = product(score[group], down(hop) + side).astype(BF16)
                send_y(hop, band).start()
            hops(go)
            go(0)

        def keep(hop):
            own_g[hop] = product(score[...].reshape(columns, rows), down(hop)).reshape(2, few, part)

        give(0, own)
        trade.wait()
        give(1, other)
        hops(keep)
        keep(0)

        def pairs(band, group):
            def go(hop):
                send_y(hop, band).wait_recv()
                out_z[hop, band] = (own_g[hop, group] + in_y[hop, band].astype(F32)).astype(BF16)
                send_z(hop, band).start()
            hops(go)

        def update(band, group):
            total = own_g.at[0, group]
            send_y(0, band).wait_recv()
            total[...] += in_y[0, band].astype(F32)

            def go(hop):
                send_z(hop, band).wait_recv()
                total[...] += in_z[hop, band].astype(F32)
            hops(go)
            stepped = shard[group] - pace[group] * (total[...] * scale_samples)
            shrunk = jnp.maximum(jnp.abs(stepped) - threshold[group], 0.0)
            fresh = jnp.where(stepped > 0, shrunk, -shrunk)
            shard[group] = fresh

            def spread_low():
                low[group, :, piece(me)] = fresh.astype(BF16)
                tell_all(low, band, group)

            def spread_change():
                change[group, :, piece(me)] = (fresh - low[group, :, piece(me)].astype(F32)).astype(BF16)
                tell_all(change, band, group)

            if first:
                spread_low()
            else:
                pl.when(turn < ITERS - 1)(spread_low)
                pl.when(turn == ITERS - 1)(spread_change)

        pairs(0, own)
        pairs(1, other)
        update(0, own)
        update(1, other)
        scattered(out_a, a_ss)
        scattered(out_b, b_ss)
        remote(out_y, out_y, y_ss, y_ss, me + side).wait_send()
        most = out_z.at[pl.ds(1, half - 1)]
        remote(most, most, z_ss, z_ss, me + side).wait_send()

    one_step(0, True)
    lax.fori_loop(1, ITERS, lambda turn, carry: (one_step(turn, False), carry)[1], 0)

    def change_keep(hop):
        span = piece(up(hop))
        return pltpu.make_async_copy(change.at[:, :, span], change_out.at[:, :, span], keep_sem.at[hop])

    def side_keep():
        span = piece(me + side)
        return pltpu.make_async_copy(change.at[:, :, span], change_out.at[:, :, span], end_sem.at[2])

    own = lax.rem(var + ITERS - 1, 2)
    change_keep(0).start()
    low_keep = pltpu.make_async_copy(low, low_out, end_sem.at[0])
    low_keep.start()
    score_wide[...] = score[...].astype(F32)
    score_keep = pltpu.make_async_copy(score_wide, score_out, end_sem.at[1])
    score_keep.start()
    pass_on(change, change_out, 0, own)
    pass_on(change, change_out, 1, 1 - own)
    hops(lambda hop: change_keep(hop).start())
    tell(change, None, 0, own).wait_recv()
    tell(change, None, 1, 1 - own).wait_recv()
    side_keep().start()
    told(change, change_out, 0, own)
    told(change, change_out, 1, 1 - own)
    low_keep.wait()
    score_keep.wait()
    change_keep(0).wait()
    hops(lambda hop: change_keep(hop).wait())
    side_keep().wait()
    hops(lambda hop: relay(change, change_out, hop, 0, own).wait_recv())
    hops(lambda hop: relay(change, change_out, hop, 1, 1 - own).wait_recv())


def local(genotypes, coefficients, time_order, fold_label, event_flag, penalty, step_size):
    rows = genotypes.shape[0]
    columns, variants = coefficients.shape
    count = lax.axis_size("samp")
    half = count // 2
    share = rows // count
    width = -(-(share + count) // 128) * 128
    total = count * width
    part = variants // count
    few = columns // 2

    def padded(value):
        return jnp.pad(value, (0, rows - columns))

    facts = jnp.stack([
        time_order.astype(F32), fold_label.astype(F32), event_flag.astype(F32), padded(step_size), padded(penalty),
    ])
    vmem = pl.BlockSpec(memory_space=pltpu.VMEM)
    away = pl.BlockSpec(memory_space=pl.ANY)
    dma = pltpu.SemaphoreType.DMA
    low, change, score = pl.pallas_call(
        functools.partial(path_kernel, count, 1.0 / math.sqrt(VARS), 1.0 / math.sqrt(rows * count)),
        out_shape=(
            jax.ShapeDtypeStruct((2, few, variants), BF16),
            jax.ShapeDtypeStruct((2, few, variants), BF16),
            jax.ShapeDtypeStruct((2, few, rows), F32),
        ),
        in_specs=[away] * 2 + [vmem],
        out_specs=(away, away, away),
        scratch_shapes=[
            pltpu.VMEM((rows, variants), BF16),
            pltpu.VMEM((columns, variants), F32),
            pltpu.VMEM((rows, total), BF16),
            pltpu.VMEM((rows, total), BF16),
            pltpu.VMEM((rows, total), BF16),
            pltpu.VMEM((rows, total), BF16),
            pltpu.VMEM((2, few, rows), F32),
            pltpu.VMEM((2, few, rows), F32),
            pltpu.VMEM((2, few, rows), F32),
            pltpu.VMEM((count, 1, width), jnp.int32),
            pltpu.VMEM((count, 1, width), jnp.int32),
            pltpu.VMEM((count, 1, width), jnp.int32),
            pltpu.VMEM((count, 8, width), F32),
            pltpu.VMEM((count, 8, width), F32),
            pltpu.VMEM((2, few, variants), BF16),
            pltpu.VMEM((2, few, variants), BF16),
            pltpu.VMEM((2, few, part), F32),
            pltpu.VMEM((2, few, 1), F32),
            pltpu.VMEM((2, few, 1), F32),
            pltpu.VMEM((2, few, rows), F32),
            pltpu.VMEM((count, few, width), F32),
            pltpu.VMEM((count, few, width), F32),
            pltpu.VMEM((count, few, width), F32),
            pltpu.VMEM((count, few, width), F32),
            pltpu.VMEM((half, 2, few, part), BF16),
            pltpu.VMEM((half, 2, few, part), BF16),
            pltpu.VMEM((half, 2, few, part), BF16),
            pltpu.VMEM((half, 2, few, part), BF16),
            pltpu.VMEM((half, 2, few, part), F32),
            pltpu.VMEM((2, few, rows), F32),
            pltpu.VMEM((few, rows), F32),
            pltpu.VMEM((2, few, rows), BF16),
            pltpu.VMEM((2, few, rows), F32),
            dma((count,)), dma, dma((3,)), dma((half,)),
            dma, dma, dma, dma((2,)),
        ] + [dma] * 6 + [dma((count,))] * 4 + [dma((half, 2))] * 6,
        compiler_params=pltpu.CompilerParams(
            collective_id=0, has_side_effects=True, vmem_limit_bytes=60 * 1024 * 1024
        ),
    )(genotypes, coefficients, facts)
    coefs = low.astype(F32) + change.astype(F32)
    return coefs.reshape(columns, variants), score.astype(BF16).reshape(columns, rows)


def solution(mesh):
    placed = (
        P("samp", "var"),
        P("pheno", "var"),
        P(("pheno", "samp")),
        P(("pheno", "samp")),
        P(("pheno", "samp")),
        P(),
        P(),
    )
    return jax.shard_map(
        local,
        mesh=mesh,
        in_specs=placed,
        out_specs=(P("pheno", "var"), P("pheno", "samp")),
        check_vma=False,
    )
```

```python
import functools
import math

import jax
import jax.numpy as jnp
from jax import lax
from jax.experimental import pallas as pl
from jax.experimental.pallas import tpu as pltpu
from jax.sharding import PartitionSpec as P

VARS = 16384
FOLDS = 8
CODES = 2 * FOLDS
ITERS = 3
MESH = pl.DeviceIdType.MESH
F32 = jnp.float32
BF16 = jnp.bfloat16


def each(count, body):
    if count <= 8:
        for step in range(count):
            body(step)
    else:
        lax.fori_loop(0, count, lambda step, carry: (body(step), carry)[1], 0)


def halves(value):
    high = value.astype(BF16)
    low = (value - high.astype(F32)).astype(BF16)
    return jnp.concatenate([high, low], axis=0)


def across(left, right):
    return lax.dot_general(left, right, (((1,), (1,)), ((), ())), preferred_element_type=F32)


def across2(value, matrix):
    rows = value.shape[0]
    both = across(halves(value), matrix)
    return both[:rows] + both[rows:]


def dot2(value, matrix):
    rows = value.shape[0]
    both = jnp.dot(halves(value), matrix, preferred_element_type=F32)
    return both[:rows] + both[rows:]


def path_kernel(
    count, scale_vars, scale_samples,
    geno_in, coef_in, codes, rates,
    low_out, change_out, score_out,
    geno, coef, to_time, later, earlier, to_id, mask, kept, kept_time, place_out, place_in, spot, code_out, code_in,
    low, change, shard, pace, threshold, half_recv, out_a, in_a, out_b, in_b,
    out_y, in_y, out_z, in_z, own_g, pred, held, score, score_wide,
    geno_sem, coef_sem, end_sem, s_ss, s_rs, half_ss, half_rs, p_ss, l_ss, a_ss, b_ss, y_ss, z_ss, c_ss, fwd_ss,
    p_rs, l_rs, a_rs, b_rs, y_rs, z_rs, c_rs, fwd_rs,
):
    me = lax.axis_index("samp")
    var = lax.axis_index("var")
    columns, variants = coef.shape
    rows = geno.shape[0]
    part = variants // count
    width = later.shape[1] // count
    share = rows // count
    half = count // 2
    few = columns // 2
    side = 1 - 2 * lax.rem(me, 2)

    def peer(step):
        return lax.rem(me + step, count)

    def down(hop):
        return lax.rem(me + 2 * hop, count)

    def up(hop):
        return lax.rem(me + count - 2 * hop, count)

    def piece(owner):
        return pl.ds(pl.multiple_of(owner * part, part), part)

    def hops(body):
        if half <= 8:
            for hop in sorted(range(1, half), key=lambda hop: (abs(2 * hop - half), hop)):
                body(hop)
        else:
            lax.fori_loop(1, half, lambda hop, carry: (body(hop), carry)[1], 0)

    def slots(owner):
        return pl.ds(pl.multiple_of(owner * width, width), width)

    def block_load(owner):
        return pltpu.make_async_copy(geno_in.at[:, piece(owner)], geno.at[:, piece(owner)], geno_sem.at[owner])

    def coef_load(owner):
        return pltpu.make_async_copy(coef_in.at[:, piece(owner)], coef.at[:, piece(owner)], coef_sem.at[owner])

    def load(owner):
        coef_load(owner).start()
        block_load(owner).start()

    each(count, load)

    barrier = pltpu.get_barrier_semaphore()

    def greet(step):
        pl.semaphore_signal(barrier, inc=1, device_id={"samp": peer(step + 1)}, device_id_type=MESH)

    each(count - 1, greet)
    pl.semaphore_signal(barrier, inc=1, device_id={"var": 1 - var}, device_id_type=MESH)

    def remote(source, target, ssem, rsem, owner):
        return pltpu.make_async_remote_copy(
            src_ref=source, dst_ref=target, send_sem=ssem, recv_sem=rsem,
            device_id={"samp": owner}, device_id_type=MESH,
        )

    def scatter(source, target, ssem, rsem):
        def push(step):
            owner = peer(step + 1)
            remote(source.at[owner], target.at[me], ssem, rsem, owner).start()
        each(count - 1, push)

    def all_in(target, rsem):
        most = target.at[pl.ds(0, count - 1)]
        remote(most, most, rsem, rsem, me + side).wait_recv()

    def arrive(target, rsem, owner):
        remote(target.at[owner], target.at[owner], rsem.at[owner], rsem.at[owner], owner).wait_recv()

    def scattered(source, ssem):
        most = source.at[pl.ds(0, count - 1)]
        remote(most, most, ssem, ssem, me + side).wait_send()

    def swap_with(source, target, ssem, rsem):
        return pltpu.make_async_remote_copy(
            src_ref=source, dst_ref=target, send_sem=ssem, recv_sem=rsem,
            device_id={"var": 1 - var}, device_id_type=MESH,
        )

    code = codes[...].reshape(1, rows)
    ids_row = (code // CODES).astype(F32)
    down_ranks = lax.broadcasted_iota(jnp.int32, (rows, rows), 0)
    along_ranks = lax.broadcasted_iota(jnp.int32, (rows, rows), 1)
    ids = jnp.sum(jnp.where(down_ranks == along_ranks, ids_row, 0.0), axis=1, keepdims=True)
    owner_row = jnp.zeros_like(ids_row)
    owner_of = jnp.zeros_like(ids)
    for owner in range(1, count):
        owner_row += jnp.where(ids_row >= owner * rows, 1.0, 0.0)
        owner_of += jnp.where(ids >= owner * rows, 1.0, 0.0)
    before = jnp.sum(
        jnp.where((owner_row == owner_of) & (along_ranks < down_ranks), 1.0, 0.0), axis=1, keepdims=True
    )
    key = (owner_of * width + before).astype(jnp.int32)
    place = (ids - owner_of * rows).astype(jnp.int32)
    ranks = lax.broadcasted_iota(jnp.int32, (rows, width), 0)
    lane = lax.broadcasted_iota(jnp.int32, (rows, width), 1)
    for owner in range(count):
        match = key == lane + owner * width
        place_out[owner] = jnp.max(jnp.where(match, place, -1), axis=0, keepdims=True)
        spot[owner] = jnp.max(jnp.where(match, ranks, -1), axis=0, keepdims=True)

    line = lax.broadcasted_iota(jnp.int32, (8, rows), 0)
    labels = jnp.where(line == 0, code % CODES // 2, jnp.where(line == 1, code % 2, 0)).astype(F32)
    column = lax.broadcasted_iota(jnp.int32, (columns, 1), 0)
    step_size = jnp.zeros((columns, 1), F32)
    least = jnp.zeros((columns, 1), F32)
    for number in range(columns):
        step_size = jnp.where(column == number, rates[number], step_size)
        least = jnp.where(column == number, rates[number] * rates[columns + number], least)
    column_fold = lax.rem(lax.broadcasted_iota(jnp.int32, (columns, rows), 0), FOLDS).astype(F32)
    trained = jnp.where(labels[0:1, :] != column_fold, 1.0, 0.0)
    counted = trained * labels[1:2, :]
    for group in range(2):
        span = slice(group * few, (group + 1) * few)
        pace[group] = step_size[span]
        threshold[group] = least[span]
        mask[group] = trained[span]
        kept[group] = counted[span]
    place_in[me] = place_out[me]

    pl.semaphore_wait(barrier, count)
    scatter(place_out, place_in, p_ss, p_rs)

    def time_block():
        block = jnp.zeros((rows, width), jnp.int32)
        for owner in range(1, count):
            block += jnp.where(place_in[owner] == ranks, owner, 0)
        return jnp.broadcast_to(jnp.sum(block, axis=1, keepdims=True), (rows, width))

    def return_map():
        block = time_block()
        for owner in range(count):
            span = slice(owner * width, (owner + 1) * width)
            hit = place_in[owner] == ranks
            to_id[:, span] = jnp.where(hit | ((lane == share) & (block > owner)), 1.0, 0.0).astype(BF16)

    def arrange():
        all_in(place_in, p_rs)
        scattered(place_out, p_ss)
        in_totals = (lane - share) == time_block()
        for owner in range(count):
            span = slice(owner * width, (owner + 1) * width)
            hit = place_in[owner] == ranks
            to_time[:, span] = jnp.where(hit | in_totals, 1.0, 0.0).astype(BF16)
        spread = jnp.dot(labels.astype(BF16), to_time[...], preferred_element_type=F32)
        for owner in range(count):
            code_out[owner] = spread[:, owner * width:(owner + 1) * width]
        scatter(code_out, code_in, l_ss, l_rs)
        code_in[me] = code_out[me]

    def sums():
        place_line = lax.broadcasted_iota(jnp.int32, (1, width), 1)
        for owner in range(count):
            span = slice(owner * width, (owner + 1) * width)
            beyond = (place_line >= share + me + 1) & (place_line < share + count)
            reach = jnp.where(beyond, rows, spot[owner])
            back = jnp.where(place_line == share, rows, spot[owner])
            later[:, span] = jnp.where(reach >= ranks, 1.0, 0.0).astype(BF16)
            earlier[:, span] = jnp.where(back >= ranks, 1.0, 0.0).astype(BF16)

    def time_labels():
        all_in(code_in, l_rs)
        scattered(code_out, l_ss)
        labels_time = jnp.zeros((labels.shape[0], rows), F32)
        for owner in range(count):
            labels_time += across(
                code_in[owner].astype(BF16), jnp.where(spot[owner] == ranks, 1.0, 0.0).astype(BF16)
            )
        counted_time = jnp.where(labels_time[0:1, :] != column_fold, 1.0, 0.0) * labels_time[1:2, :]
        for group in range(2):
            kept_time[group] = counted_time[group * few:(group + 1) * few]

    def tell(held_in, hop, band, group):
        block = held_in.at[group, :, piece(me)]
        owner = me + side if hop is None else down(hop)
        index = (0 if hop is None else hop, band)
        return remote(block, block, c_ss, c_rs.at[index], owner)

    def relay(held_in, end, hop, band, group):
        span = piece(up(hop))
        return remote(
            held_in.at[group, :, span], end.at[group, :, span], fwd_ss, fwd_rs.at[hop, band], me + side
        )

    def tell_all(held_in, band, group):
        hops(lambda hop: tell(held_in, hop, band, group).start())
        tell(held_in, None, band, group).start()

    def pass_on(held_in, end, band, group):
        def go(hop):
            tell(held_in, hop, band, group).wait_recv()
            relay(held_in, end, hop, band, group).start()
        hops(go)

    def told():
        sent = low.at[:, :, pl.ds(0, half * part)]
        remote(sent, sent, c_ss, c_ss, me + side).wait_send()
        sent = low.at[:, :, pl.ds(0, (half - 1) * part)]
        remote(sent, sent, fwd_ss, fwd_ss, me + side).wait_send()

    upper = jnp.where(2 * me >= count, 1, 0)

    def far(step):
        return lax.rem(me + jnp.where(upper == 1, step + 1, count - 1 - step), count)

    def spread_far(value, matrix, source, target, ssem, rsem):
        split = halves(value)
        near = upper * half

        def block(first):
            span = pl.ds(pl.multiple_of(first * width, width), half * width)
            both = jnp.dot(split, matrix[:, span], preferred_element_type=F32)
            block = both[:few] + both[few:]
            for owner in range(half):
                source[first + owner] = block[:, owner * width:(owner + 1) * width]

        def push(owner):
            remote(source.at[owner], target.at[me], ssem, rsem.at[me], owner).start()

        block(half - near)
        each(half, lambda step: push(lax.rem(half - near + lax.rem(me + step, half), count)))
        block(near)
        each(half - 1, lambda step: push(near + lax.rem(me + step + 1, half)))

    def gather_far(source, target, rsem, matrix):
        total = across2(source[me], matrix[:, slots(me)])
        for step in range(count - 1):
            owner = far(count - 2 - step)
            arrive(target, rsem, owner)
            total += across2(target[owner], matrix[:, slots(owner)])
        return total

    def send_y(hop, band):
        return remote(out_y.at[hop, band], in_y.at[hop, band], y_ss, y_rs.at[hop, band], me + side)

    def send_z(hop, band):
        return remote(out_z.at[hop, band], in_z.at[hop, band], z_ss, z_rs.at[hop, band], down(hop))

    def add_part(owner, group):
        pred[group] += across(low[group, :, piece(owner)], geno[:, piece(owner)])

    def both_parts(owner):
        both = across(low[:, :, piece(owner)].reshape(columns, part), geno[:, piece(owner)])
        return both.reshape(2, few, rows)

    def one_step(turn, first):
        own = lax.rem(var + turn, 2)
        other = 1 - own
        slot = lax.rem(turn, 2)
        swap = swap_with(pred.at[other], half_recv.at[slot], half_ss, half_rs.at[slot])
        if first:
            pred[...] = jnp.zeros_like(pred)

            def add_block(owner):
                coef_load(owner).wait()
                for group in range(2):
                    low[group, :, piece(owner)] = coef[group * few:(group + 1) * few, piece(owner)].astype(BF16)
                block_load(owner).wait()
                pred[...] += both_parts(owner)
            each(count, add_block)
            swap.start()
            for group in range(2):
                shard[group] = coef[group * few:(group + 1) * few, piece(me)]
            arrange()
        else:
            def add_side(band, group):
                def go(hop):
                    relay(low, low, hop, band, group).wait_recv()
                    add_part(up(hop) + side, group)
                hops(go)

            pred[...] = both_parts(me)
            pass_on(low, low, 0, other)
            tell(low, None, 0, other).wait_recv()
            tell(low, None, 1, own).wait_recv()
            pred[...] += both_parts(me + side)
            hops(lambda hop: add_part(up(hop), other))
            pass_on(low, low, 1, own)
            add_side(0, other)
            swap.start()
            hops(lambda hop: add_part(up(hop), own))
            add_side(1, own)
            told()
        swap.wait()

        weight = mask[own] * jnp.exp((pred[own] + half_recv[slot]) * scale_vars)
        held[...] = weight
        spread_far(weight, to_time, out_a, in_a, a_ss, a_rs)
        if first:
            sums()
            time_labels()
        total = gather_far(out_a, in_a, a_rs, later)
        events = kept_time[own]
        ratio = events / jnp.where(events > 0, total, 1.0)
        spread_far(ratio, earlier, out_b, in_b, b_ss, b_rs)
        if first:
            return_map()
        total = gather_far(out_b, in_b, b_rs, to_id)
        score[own] = (held[...] * total - kept[own]).astype(BF16)
        trade = swap_with(score.at[own], score.at[own], s_ss, s_rs)
        trade.start()

        def product(left, owner):
            return jnp.dot(left, geno[:, piece(owner)], preferred_element_type=F32)

        def give(band, group):
            def go(hop):
                out_y[hop, band] = product(score[group], down(hop) + side).astype(BF16)
                send_y(hop, band).start()
            hops(go)

        def keep(group):
            def go(hop):
                own_g[hop, group] = product(score[group], down(hop))
            hops(go)

        def pairs(band, group):
            def go(hop):
                send_y(hop, band).wait_recv()
                out_z[hop, band] = (own_g[hop, group] + in_y[hop, band].astype(F32)).astype(BF16)
                send_z(hop, band).start()
            hops(go)

        give(0, own)
        keep(own)
        trade.wait()
        give(1, other)
        pairs(0, own)
        out_y[0] = product(score[...].reshape(columns, rows), me + side).reshape(2, few, part).astype(BF16)
        send_y(0, own).start()
        send_y(0, other).start()
        keep(other)
        pairs(1, other)
        own_g[0] = product(score[...].reshape(columns, rows), me).reshape(2, few, part)

        def update(band, group):
            total = own_g.at[0, group]
            send_y(0, group).wait_recv()
            total[...] += in_y[0, group].astype(F32)

            def go(hop):
                send_z(hop, band).wait_recv()
                total[...] += in_z[hop, band].astype(F32)
            hops(go)
            stepped = shard[group] - pace[group] * (total[...] * scale_samples)
            shrunk = jnp.maximum(jnp.abs(stepped) - threshold[group], 0.0)
            fresh = jnp.where(stepped > 0, shrunk, -shrunk)
            shard[group] = fresh

            def spread_low():
                low[group, :, piece(me)] = fresh.astype(BF16)
                tell_all(low, band, group)

            def spread_change():
                change[group, :, piece(me)] = (fresh - low[group, :, piece(me)].astype(F32)).astype(BF16)
                tell_all(change, band, group)

            if first:
                spread_low()
            else:
                pl.when(turn < ITERS - 1)(spread_low)
                pl.when(turn == ITERS - 1)(spread_change)

        update(0, own)
        update(1, other)
        scattered(out_a, a_ss)
        scattered(out_b, b_ss)
        remote(out_y, out_y, y_ss, y_ss, me + side).wait_send()
        most = out_z.at[pl.ds(1, half - 1)]
        remote(most, most, z_ss, z_ss, me + side).wait_send()

    one_step(0, True)
    lax.fori_loop(1, ITERS, lambda turn, carry: (one_step(turn, False), carry)[1], 0)

    def keep_change(owner):
        span = piece(owner)
        pltpu.make_async_copy(change.at[:, :, span], change_out.at[:, :, span], end_sem.at[2]).start()

    own = lax.rem(var + ITERS - 1, 2)
    keep_change(me)
    low_keep = pltpu.make_async_copy(low, low_out, end_sem.at[0])
    low_keep.start()
    score_wide[...] = score[...].astype(F32)
    score_keep = pltpu.make_async_copy(score_wide, score_out, end_sem.at[1])
    score_keep.start()
    pass_on(change, change_out, 0, own)
    pass_on(change, change_out, 1, 1 - own)
    hops(lambda hop: keep_change(up(hop)))
    tell(change, None, 0, own).wait_recv()
    tell(change, None, 1, 1 - own).wait_recv()
    keep_change(me + side)
    told()
    low_keep.wait()
    score_keep.wait()
    kept_change = pl.ds(0, (half + 1) * part)
    pltpu.make_async_copy(change.at[:, :, kept_change], change_out.at[:, :, kept_change], end_sem.at[2]).wait()
    hops(lambda hop: relay(change, change_out, hop, 0, own).wait_recv())
    hops(lambda hop: relay(change, change_out, hop, 1, 1 - own).wait_recv())


def local(genotypes, coefficients, time_order, fold_label, event_flag, penalty, step_size):
    rows = genotypes.shape[0]
    columns, variants = coefficients.shape
    count = lax.axis_size("samp")
    half = count // 2
    share = rows // count
    width = -(-(share + count) // 128) * 128
    total = count * width
    part = variants // count
    few = columns // 2

    codes = time_order * CODES + fold_label * 2 + event_flag
    vmem = pl.BlockSpec(memory_space=pltpu.VMEM)
    away = pl.BlockSpec(memory_space=pl.ANY)
    hbm = pl.BlockSpec(memory_space=pltpu.HBM)
    dma = pltpu.SemaphoreType.DMA
    low, change, score = pl.pallas_call(
        functools.partial(path_kernel, count, 1.0 / math.sqrt(VARS), 1.0 / math.sqrt(rows * count)),
        out_shape=(
            jax.ShapeDtypeStruct((2, few, variants), BF16),
            jax.ShapeDtypeStruct((2, few, variants), BF16),
            jax.ShapeDtypeStruct((2, few, rows), F32),
        ),
        in_specs=[hbm] * 2 + [vmem] + [pl.BlockSpec(memory_space=pltpu.SMEM)],
        out_specs=(away, away, away),
        scratch_shapes=[
            pltpu.VMEM((rows, variants), BF16),
            pltpu.VMEM((columns, variants), F32),
            pltpu.VMEM((rows, total), BF16),
            pltpu.VMEM((rows, total), BF16),
            pltpu.VMEM((rows, total), BF16),
            pltpu.VMEM((rows, total), BF16),
            pltpu.VMEM((2, few, rows), F32),
            pltpu.VMEM((2, few, rows), F32),
            pltpu.VMEM((2, few, rows), F32),
            pltpu.VMEM((count, 1, width), jnp.int32),
            pltpu.VMEM((count, 1, width), jnp.int32),
            pltpu.VMEM((count, 1, width), jnp.int32),
            pltpu.VMEM((count, 8, width), F32),
            pltpu.VMEM((count, 8, width), F32),
            pltpu.VMEM((2, few, variants), BF16),
            pltpu.VMEM((2, few, variants), BF16),
            pltpu.VMEM((2, few, part), F32),
            pltpu.VMEM((2, few, 1), F32),
            pltpu.VMEM((2, few, 1), F32),
            pltpu.VMEM((2, few, rows), F32),
            pltpu.VMEM((count, few, width), F32),
            pltpu.VMEM((count, few, width), F32),
            pltpu.VMEM((count, few, width), F32),
            pltpu.VMEM((count, few, width), F32),
            pltpu.VMEM((half, 2, few, part), BF16),
            pltpu.VMEM((half, 2, few, part), BF16),
            pltpu.VMEM((half, 2, few, part), BF16),
            pltpu.VMEM((half, 2, few, part), BF16),
            pltpu.VMEM((half, 2, few, part), F32),
            pltpu.VMEM((2, few, rows), F32),
            pltpu.VMEM((few, rows), F32),
            pltpu.VMEM((2, few, rows), BF16),
            pltpu.VMEM((2, few, rows), F32),
            dma((count,)), dma((count,)), dma((3,)),
            dma, dma, dma, dma((2,)),
        ] + [dma] * 10 + [dma((count,))] * 2 + [dma((half, 2))] * 4,
        compiler_params=pltpu.CompilerParams(
            collective_id=0, has_side_effects=True, vmem_limit_bytes=52 * 1024 * 1024
        ),
    )(genotypes, coefficients, codes, jnp.concatenate([step_size, penalty]))
    coefs = low.astype(F32) + change.astype(F32)
    return coefs.reshape(columns, variants), score.astype(BF16).reshape(columns, rows)


def solution(mesh):
    placed = (
        P("samp", "var"),
        P("pheno", "var"),
        P(("pheno", "samp")),
        P(("pheno", "samp")),
        P(("pheno", "samp")),
        P(),
        P(),
    )
    return jax.shard_map(
        local,
        mesh=mesh,
        in_specs=placed,
        out_specs=(P("pheno", "var"), P("pheno", "samp")),
        check_vma=False,
    )
```

```python
import functools
import math

import jax
import jax.numpy as jnp
from jax import lax
from jax.experimental import pallas as pl
from jax.experimental.pallas import tpu as pltpu
from jax.sharding import PartitionSpec as P

VARS = 16384
FOLDS = 8
CODES = 2 * FOLDS
ITERS = 3
MESH = pl.DeviceIdType.MESH
F32 = jnp.float32
BF16 = jnp.bfloat16


def each(count, body):
    if count <= 8:
        for step in range(count):
            body(step)
    else:
        lax.fori_loop(0, count, lambda step, carry: (body(step), carry)[1], 0)


def halves(value):
    high = value.astype(BF16)
    low = (value - high.astype(F32)).astype(BF16)
    return jnp.concatenate([high, low], axis=0)


def across(left, right):
    return lax.dot_general(left, right, (((1,), (1,)), ((), ())), preferred_element_type=F32)


def across2(value, matrix):
    rows = value.shape[0]
    both = across(halves(value), matrix)
    return both[:rows] + both[rows:]


def dot2(value, matrix):
    rows = value.shape[0]
    both = jnp.dot(halves(value), matrix, preferred_element_type=F32)
    return both[:rows] + both[rows:]


def path_kernel(
    count, scale_vars, scale_samples,
    geno_in, coef_in, facts,
    low_out, change_out, score_out,
    geno, coef, to_time, later, earlier, to_id, mask, kept, kept_time, place_out, place_in, spot, code_out, code_in,
    low, change, shard, pace, threshold, half_recv, out_a, in_a, out_b, in_b,
    out_y, in_y, out_z, in_z, own_g, pred, held, score, score_wide,
    geno_sem, coef_sem, end_sem, s_ss, s_rs, half_ss, half_rs, p_ss, l_ss, a_ss, b_ss, y_ss, z_ss, c_ss, fwd_ss,
    p_rs, l_rs, a_rs, b_rs, y_rs, z_rs, c_rs, fwd_rs,
):
    me = lax.axis_index("samp")
    var = lax.axis_index("var")
    columns, variants = coef.shape
    rows = geno.shape[0]
    part = variants // count
    width = later.shape[1] // count
    share = rows // count
    half = count // 2
    few = columns // 2
    side = 1 - 2 * lax.rem(me, 2)

    def peer(step):
        return lax.rem(me + step, count)

    def down(hop):
        return lax.rem(me + 2 * hop, count)

    def up(hop):
        return lax.rem(me + count - 2 * hop, count)

    def piece(owner):
        return pl.ds(pl.multiple_of(owner * part, part), part)

    def hops(body):
        if half <= 8:
            for hop in sorted(range(1, half), key=lambda hop: (abs(2 * hop - half), hop)):
                body(hop)
        else:
            lax.fori_loop(1, half, lambda hop, carry: (body(hop), carry)[1], 0)

    def slots(owner):
        return pl.ds(pl.multiple_of(owner * width, width), width)

    def block_load(owner):
        return pltpu.make_async_copy(geno_in.at[:, piece(owner)], geno.at[:, piece(owner)], geno_sem.at[owner])

    def coef_load(owner):
        return pltpu.make_async_copy(coef_in.at[:, piece(owner)], coef.at[:, piece(owner)], coef_sem.at[owner])

    def load(owner):
        coef_load(owner).start()
        block_load(owner).start()

    each(count, load)

    barrier = pltpu.get_barrier_semaphore()

    def greet(step):
        pl.semaphore_signal(barrier, inc=1, device_id={"samp": peer(step + 1)}, device_id_type=MESH)

    each(count - 1, greet)
    pl.semaphore_signal(barrier, inc=1, device_id={"var": 1 - var}, device_id_type=MESH)

    def remote(source, target, ssem, rsem, owner):
        return pltpu.make_async_remote_copy(
            src_ref=source, dst_ref=target, send_sem=ssem, recv_sem=rsem,
            device_id={"samp": owner}, device_id_type=MESH,
        )

    def scatter(source, target, ssem, rsem):
        def push(step):
            owner = peer(step + 1)
            remote(source.at[owner], target.at[me], ssem, rsem, owner).start()
        each(count - 1, push)

    def all_in(target, rsem):
        most = target.at[pl.ds(0, count - 1)]
        remote(most, most, rsem, rsem, me + side).wait_recv()

    def arrive(target, rsem, owner):
        remote(target.at[owner], target.at[owner], rsem.at[owner], rsem.at[owner], owner).wait_recv()

    def scattered(source, ssem):
        most = source.at[pl.ds(0, count - 1)]
        remote(most, most, ssem, ssem, me + side).wait_send()

    def swap_with(source, target, ssem, rsem):
        return pltpu.make_async_remote_copy(
            src_ref=source, dst_ref=target, send_sem=ssem, recv_sem=rsem,
            device_id={"var": 1 - var}, device_id_type=MESH,
        )

    fact = facts[...].reshape(1, rows + 2 * columns)
    code = fact[:, :rows].astype(jnp.int32)
    ids_row = (code // CODES).astype(F32)
    down_ranks = lax.broadcasted_iota(jnp.int32, (rows, rows), 0)
    along_ranks = lax.broadcasted_iota(jnp.int32, (rows, rows), 1)
    ids = jnp.sum(jnp.where(down_ranks == along_ranks, ids_row, 0.0), axis=1, keepdims=True)
    owner_row = jnp.zeros_like(ids_row)
    owner_of = jnp.zeros_like(ids)
    for owner in range(1, count):
        owner_row += jnp.where(ids_row >= owner * rows, 1.0, 0.0)
        owner_of += jnp.where(ids >= owner * rows, 1.0, 0.0)
    before = jnp.sum(
        jnp.where((owner_row == owner_of) & (along_ranks < down_ranks), 1.0, 0.0), axis=1, keepdims=True
    )
    key = (owner_of * width + before).astype(jnp.int32)
    place = (ids - owner_of * rows).astype(jnp.int32)
    ranks = lax.broadcasted_iota(jnp.int32, (rows, width), 0)
    lane = lax.broadcasted_iota(jnp.int32, (rows, width), 1)
    for owner in range(count):
        match = key == lane + owner * width
        place_out[owner] = jnp.max(jnp.where(match, place, -1), axis=0, keepdims=True)
        spot[owner] = jnp.max(jnp.where(match, ranks, -1), axis=0, keepdims=True)

    line = lax.broadcasted_iota(jnp.int32, (8, rows), 0)
    labels = jnp.where(line == 0, code % CODES // 2, jnp.where(line == 1, code % 2, 0)).astype(F32)
    column = lax.broadcasted_iota(jnp.int32, (columns, 2 * columns), 0)
    number = lax.broadcasted_iota(jnp.int32, (columns, 2 * columns), 1)
    rates = fact[:, rows:]
    step_size = jnp.sum(jnp.where(number == column, rates, 0.0), axis=1, keepdims=True)
    least = step_size * jnp.sum(jnp.where(number == column + columns, rates, 0.0), axis=1, keepdims=True)
    column_fold = lax.rem(lax.broadcasted_iota(jnp.int32, (columns, rows), 0), FOLDS).astype(F32)
    trained = jnp.where(labels[0:1, :] != column_fold, 1.0, 0.0)
    counted = trained * labels[1:2, :]
    for group in range(2):
        span = slice(group * few, (group + 1) * few)
        pace[group] = step_size[span]
        threshold[group] = least[span]
        mask[group] = trained[span]
        kept[group] = counted[span]
    place_in[me] = place_out[me]

    pl.semaphore_wait(barrier, count)
    scatter(place_out, place_in, p_ss, p_rs)

    def time_block():
        block = jnp.zeros((rows, width), jnp.int32)
        for owner in range(1, count):
            block += jnp.where(place_in[owner] == ranks, owner, 0)
        return jnp.broadcast_to(jnp.sum(block, axis=1, keepdims=True), (rows, width))

    def return_map():
        block = time_block()
        for owner in range(count):
            span = slice(owner * width, (owner + 1) * width)
            hit = place_in[owner] == ranks
            to_id[:, span] = jnp.where(hit | ((lane == share) & (block > owner)), 1.0, 0.0).astype(BF16)

    def arrange():
        all_in(place_in, p_rs)
        scattered(place_out, p_ss)
        in_totals = (lane - share) == time_block()
        for owner in range(count):
            span = slice(owner * width, (owner + 1) * width)
            hit = place_in[owner] == ranks
            to_time[:, span] = jnp.where(hit | in_totals, 1.0, 0.0).astype(BF16)
        spread = jnp.dot(labels.astype(BF16), to_time[...], preferred_element_type=F32)
        for owner in range(count):
            code_out[owner] = spread[:, owner * width:(owner + 1) * width]
        scatter(code_out, code_in, l_ss, l_rs)
        code_in[me] = code_out[me]

    def sums():
        place_line = lax.broadcasted_iota(jnp.int32, (1, width), 1)
        for owner in range(count):
            span = slice(owner * width, (owner + 1) * width)
            beyond = (place_line >= share + me + 1) & (place_line < share + count)
            reach = jnp.where(beyond, rows, spot[owner])
            back = jnp.where(place_line == share, rows, spot[owner])
            later[:, span] = jnp.where(reach >= ranks, 1.0, 0.0).astype(BF16)
            earlier[:, span] = jnp.where(back >= ranks, 1.0, 0.0).astype(BF16)

    def time_labels():
        all_in(code_in, l_rs)
        scattered(code_out, l_ss)
        labels_time = jnp.zeros((labels.shape[0], rows), F32)
        for owner in range(count):
            labels_time += across(
                code_in[owner].astype(BF16), jnp.where(spot[owner] == ranks, 1.0, 0.0).astype(BF16)
            )
        counted_time = jnp.where(labels_time[0:1, :] != column_fold, 1.0, 0.0) * labels_time[1:2, :]
        for group in range(2):
            kept_time[group] = counted_time[group * few:(group + 1) * few]

    def tell(held_in, hop, band, group):
        block = held_in.at[group, :, piece(me)]
        owner = me + side if hop is None else down(hop)
        index = (0 if hop is None else hop, band)
        return remote(block, block, c_ss, c_rs.at[index], owner)

    def relay(held_in, end, hop, band, group):
        span = piece(up(hop))
        return remote(
            held_in.at[group, :, span], end.at[group, :, span], fwd_ss, fwd_rs.at[hop, band], me + side
        )

    def tell_all(held_in, band, group):
        hops(lambda hop: tell(held_in, hop, band, group).start())
        tell(held_in, None, band, group).start()

    def pass_on(held_in, end, band, group):
        def go(hop):
            tell(held_in, hop, band, group).wait_recv()
            relay(held_in, end, hop, band, group).start()
        hops(go)

    def told():
        sent = low.at[:, :, pl.ds(0, half * part)]
        remote(sent, sent, c_ss, c_ss, me + side).wait_send()
        sent = low.at[:, :, pl.ds(0, (half - 1) * part)]
        remote(sent, sent, fwd_ss, fwd_ss, me + side).wait_send()

    upper = jnp.where(2 * me >= count, 1, 0)

    def far(step):
        return lax.rem(me + jnp.where(upper == 1, step + 1, count - 1 - step), count)

    def spread_far(value, matrix, source, target, ssem, rsem):
        split = halves(value)
        near = upper * half

        def block(first):
            span = pl.ds(pl.multiple_of(first * width, width), half * width)
            both = jnp.dot(split, matrix[:, span], preferred_element_type=F32)
            block = both[:few] + both[few:]
            for owner in range(half):
                source[first + owner] = block[:, owner * width:(owner + 1) * width]

        def push(owner):
            remote(source.at[owner], target.at[me], ssem, rsem.at[me], owner).start()

        block(half - near)
        each(half, lambda step: push(lax.rem(half - near + lax.rem(me + step, half), count)))
        block(near)
        each(half - 1, lambda step: push(near + lax.rem(me + step + 1, half)))

    def gather_far(source, target, rsem, matrix):
        total = across2(source[me], matrix[:, slots(me)])
        for step in range(count - 1):
            owner = far(count - 2 - step)
            arrive(target, rsem, owner)
            total += across2(target[owner], matrix[:, slots(owner)])
        return total

    def send_y(hop, band):
        return remote(out_y.at[hop, band], in_y.at[hop, band], y_ss, y_rs.at[hop, band], me + side)

    def send_z(hop, band):
        return remote(out_z.at[hop, band], in_z.at[hop, band], z_ss, z_rs.at[hop, band], down(hop))

    def add_part(owner, group):
        pred[group] += across(low[group, :, piece(owner)], geno[:, piece(owner)])

    def both_parts(owner):
        both = across(low[:, :, piece(owner)].reshape(columns, part), geno[:, piece(owner)])
        return both.reshape(2, few, rows)

    def one_step(turn, first):
        own = lax.rem(var + turn, 2)
        other = 1 - own
        slot = lax.rem(turn, 2)
        swap = swap_with(pred.at[other], half_recv.at[slot], half_ss, half_rs.at[slot])
        if first:
            pred[...] = jnp.zeros_like(pred)

            def add_block(owner):
                coef_load(owner).wait()
                for group in range(2):
                    low[group, :, piece(owner)] = coef[group * few:(group + 1) * few, piece(owner)].astype(BF16)
                block_load(owner).wait()
                pred[...] += both_parts(owner)
            each(count, add_block)
            swap.start()
            for group in range(2):
                shard[group] = coef[group * few:(group + 1) * few, piece(me)]
            arrange()
        else:
            def add_side(band, group):
                def go(hop):
                    relay(low, low, hop, band, group).wait_recv()
                    add_part(up(hop) + side, group)
                hops(go)

            pred[...] = both_parts(me)
            pass_on(low, low, 0, other)
            tell(low, None, 0, other).wait_recv()
            tell(low, None, 1, own).wait_recv()
            pred[...] += both_parts(me + side)
            pass_on(low, low, 1, own)

            def add_up(hop):
                pred[...] += both_parts(up(hop))
            hops(add_up)
            add_side(0, other)
            swap.start()
            add_side(1, own)
            told()
        swap.wait()

        weight = mask[own] * jnp.exp((pred[own] + half_recv[slot]) * scale_vars)
        held[...] = weight
        spread_far(weight, to_time, out_a, in_a, a_ss, a_rs)
        if first:
            sums()
            time_labels()
        total = gather_far(out_a, in_a, a_rs, later)
        events = kept_time[own]
        ratio = events / jnp.where(events > 0, total, 1.0)
        spread_far(ratio, earlier, out_b, in_b, b_ss, b_rs)
        if first:
            return_map()
        total = gather_far(out_b, in_b, b_rs, to_id)
        score[own] = (held[...] * total - kept[own]).astype(BF16)
        trade = swap_with(score.at[own], score.at[own], s_ss, s_rs)
        trade.start()

        def product(left, owner):
            return jnp.dot(left, geno[:, piece(owner)], preferred_element_type=F32)

        def give(band, group):
            def go(hop):
                out_y[hop, band] = product(score[group], down(hop) + side).astype(BF16)
                send_y(hop, band).start()
            hops(go)

        def keep(group):
            def go(hop):
                own_g[hop, group] = product(score[group], down(hop))
            hops(go)

        def pairs(band, group):
            def go(hop):
                send_y(hop, band).wait_recv()
                out_z[hop, band] = (own_g[hop, group] + in_y[hop, band].astype(F32)).astype(BF16)
                send_z(hop, band).start()
            hops(go)

        give(0, own)
        keep(own)
        trade.wait()
        give(1, other)
        pairs(0, own)
        out_y[0] = product(score[...].reshape(columns, rows), me + side).reshape(2, few, part).astype(BF16)
        send_y(0, own).start()
        send_y(0, other).start()
        keep(other)
        pairs(1, other)
        own_g[0] = product(score[...].reshape(columns, rows), me).reshape(2, few, part)

        def update(band, group):
            total = own_g.at[0, group]
            send_y(0, group).wait_recv()
            total[...] += in_y[0, group].astype(F32)

            def go(hop):
                send_z(hop, band).wait_recv()
                total[...] += in_z[hop, band].astype(F32)
            hops(go)
            stepped = shard[group] - pace[group] * (total[...] * scale_samples)
            shrunk = jnp.maximum(jnp.abs(stepped) - threshold[group], 0.0)
            fresh = jnp.where(stepped > 0, shrunk, -shrunk)
            shard[group] = fresh

            def spread_low():
                low[group, :, piece(me)] = fresh.astype(BF16)
                tell_all(low, band, group)

            def spread_change():
                change[group, :, piece(me)] = (fresh - low[group, :, piece(me)].astype(F32)).astype(BF16)
                tell_all(change, band, group)

            if first:
                spread_low()
            else:
                pl.when(turn < ITERS - 1)(spread_low)
                pl.when(turn == ITERS - 1)(spread_change)

        update(0, own)
        update(1, other)
        scattered(out_a, a_ss)
        scattered(out_b, b_ss)
        remote(out_y, out_y, y_ss, y_ss, me + side).wait_send()
        most = out_z.at[pl.ds(1, half - 1)]
        remote(most, most, z_ss, z_ss, me + side).wait_send()

    one_step(0, True)
    lax.fori_loop(1, ITERS, lambda turn, carry: (one_step(turn, False), carry)[1], 0)

    def keep_change(owner):
        span = piece(owner)
        pltpu.make_async_copy(change.at[:, :, span], change_out.at[:, :, span], end_sem.at[2]).start()

    own = lax.rem(var + ITERS - 1, 2)
    keep_change(me)
    low_keep = pltpu.make_async_copy(low, low_out, end_sem.at[0])
    low_keep.start()
    score_wide[...] = score[...].astype(F32)
    score_keep = pltpu.make_async_copy(score_wide, score_out, end_sem.at[1])
    score_keep.start()
    pass_on(change, change_out, 0, own)
    pass_on(change, change_out, 1, 1 - own)
    hops(lambda hop: keep_change(up(hop)))
    tell(change, None, 0, own).wait_recv()
    tell(change, None, 1, 1 - own).wait_recv()
    keep_change(me + side)
    told()
    low_keep.wait()
    score_keep.wait()
    kept_change = pl.ds(0, (half + 1) * part)
    pltpu.make_async_copy(change.at[:, :, kept_change], change_out.at[:, :, kept_change], end_sem.at[2]).wait()
    hops(lambda hop: relay(change, change_out, hop, 0, own).wait_recv())
    hops(lambda hop: relay(change, change_out, hop, 1, 1 - own).wait_recv())


def local(genotypes, coefficients, time_order, fold_label, event_flag, penalty, step_size):
    rows = genotypes.shape[0]
    columns, variants = coefficients.shape
    count = lax.axis_size("samp")
    half = count // 2
    share = rows // count
    width = -(-(share + count) // 128) * 128
    total = count * width
    part = variants // count
    few = columns // 2

    codes = time_order * CODES + fold_label * 2 + event_flag
    facts = jnp.concatenate([codes.astype(F32), step_size, penalty])
    vmem = pl.BlockSpec(memory_space=pltpu.VMEM)
    away = pl.BlockSpec(memory_space=pl.ANY)
    hbm = pl.BlockSpec(memory_space=pltpu.HBM)
    dma = pltpu.SemaphoreType.DMA
    low, change, score = pl.pallas_call(
        functools.partial(path_kernel, count, 1.0 / math.sqrt(VARS), 1.0 / math.sqrt(rows * count)),
        out_shape=(
            jax.ShapeDtypeStruct((2, few, variants), BF16),
            jax.ShapeDtypeStruct((2, few, variants), BF16),
            jax.ShapeDtypeStruct((2, few, rows), F32),
        ),
        in_specs=[hbm] * 2 + [vmem],
        out_specs=(away, away, away),
        scratch_shapes=[
            pltpu.VMEM((rows, variants), BF16),
            pltpu.VMEM((columns, variants), F32),
            pltpu.VMEM((rows, total), BF16),
            pltpu.VMEM((rows, total), BF16),
            pltpu.VMEM((rows, total), BF16),
            pltpu.VMEM((rows, total), BF16),
            pltpu.VMEM((2, few, rows), F32),
            pltpu.VMEM((2, few, rows), F32),
            pltpu.VMEM((2, few, rows), F32),
            pltpu.VMEM((count, 1, width), jnp.int32),
            pltpu.VMEM((count, 1, width), jnp.int32),
            pltpu.VMEM((count, 1, width), jnp.int32),
            pltpu.VMEM((count, 8, width), F32),
            pltpu.VMEM((count, 8, width), F32),
            pltpu.VMEM((2, few, variants), BF16),
            pltpu.VMEM((2, few, variants), BF16),
            pltpu.VMEM((2, few, part), F32),
            pltpu.VMEM((2, few, 1), F32),
            pltpu.VMEM((2, few, 1), F32),
            pltpu.VMEM((2, few, rows), F32),
            pltpu.VMEM((count, few, width), F32),
            pltpu.VMEM((count, few, width), F32),
            pltpu.VMEM((count, few, width), F32),
            pltpu.VMEM((count, few, width), F32),
            pltpu.VMEM((half, 2, few, part), BF16),
            pltpu.VMEM((half, 2, few, part), BF16),
            pltpu.VMEM((half, 2, few, part), BF16),
            pltpu.VMEM((half, 2, few, part), BF16),
            pltpu.VMEM((half, 2, few, part), F32),
            pltpu.VMEM((2, few, rows), F32),
            pltpu.VMEM((few, rows), F32),
            pltpu.VMEM((2, few, rows), BF16),
            pltpu.VMEM((2, few, rows), F32),
            dma((count,)), dma((count,)), dma((3,)),
            dma, dma, dma, dma((2,)),
        ] + [dma] * 10 + [dma((count,))] * 2 + [dma((half, 2))] * 4,
        compiler_params=pltpu.CompilerParams(
            collective_id=0, has_side_effects=True, vmem_limit_bytes=52 * 1024 * 1024
        ),
    )(genotypes, coefficients, facts)
    coefs = low.astype(F32) + change.astype(F32)
    return coefs.reshape(columns, variants), score.astype(BF16).reshape(columns, rows)


def solution(mesh):
    placed = (
        P("samp", "var"),
        P("pheno", "var"),
        P(("pheno", "samp")),
        P(("pheno", "samp")),
        P(("pheno", "samp")),
        P(),
        P(),
    )
    return jax.shard_map(
        local,
        mesh=mesh,
        in_specs=placed,
        out_specs=(P("pheno", "var"), P("pheno", "samp")),
        check_vma=False,
    )
```

```python
import functools
import math

import jax
import jax.numpy as jnp
from jax import lax
from jax.experimental import pallas as pl
from jax.experimental.pallas import tpu as pltpu
from jax.sharding import PartitionSpec as P

VARS = 16384
FOLDS = 8
CODES = 2 * FOLDS
ITERS = 3
MESH = pl.DeviceIdType.MESH
F32 = jnp.float32
BF16 = jnp.bfloat16


def each(count, body):
    if count <= 8:
        for step in range(count):
            body(step)
    else:
        lax.fori_loop(0, count, lambda step, carry: (body(step), carry)[1], 0)


def halves(value):
    high = value.astype(BF16)
    low = (value - high.astype(F32)).astype(BF16)
    return jnp.concatenate([high, low], axis=0)


def across(left, right):
    return lax.dot_general(left, right, (((1,), (1,)), ((), ())), preferred_element_type=F32)


def across2(value, matrix):
    rows = value.shape[0]
    both = across(halves(value), matrix)
    return both[:rows] + both[rows:]


def dot2(value, matrix):
    rows = value.shape[0]
    both = jnp.dot(halves(value), matrix, preferred_element_type=F32)
    return both[:rows] + both[rows:]


def path_kernel(
    count, scale_vars, scale_samples,
    geno_in, coef_in, facts,
    low_out, change_out, score_out,
    geno, coef, to_time, later, earlier, to_id, mask, kept, kept_time, place_out, place_in, spot, code_out, code_in,
    low, change, shard, pace, threshold, half_recv, out_a, in_a, out_b, in_b,
    out_y, in_y, out_z, in_z, own_g, pred, held, score, score_wide,
    geno_sem, coef_sem, end_sem, s_ss, s_rs, half_ss, half_rs, p_ss, l_ss, a_ss, b_ss, y_ss, z_ss, c_ss, fwd_ss,
    p_rs, l_rs, a_rs, b_rs, y_rs, z_rs, c_rs, fwd_rs,
):
    me = lax.axis_index("samp")
    var = lax.axis_index("var")
    columns, variants = coef.shape
    rows = geno.shape[0]
    part = variants // count
    width = later.shape[1] // count
    share = rows // count
    half = count // 2
    few = columns // 2
    side = 1 - 2 * lax.rem(me, 2)

    def peer(step):
        return lax.rem(me + step, count)

    def down(hop):
        return lax.rem(me + 2 * hop, count)

    def up(hop):
        return lax.rem(me + count - 2 * hop, count)

    def piece(owner):
        return pl.ds(pl.multiple_of(owner * part, part), part)

    def hops(body, order=(2, 1, 3)):
        if half <= 8:
            for hop in (order if half == 4 else range(1, half)):
                body(hop)
        else:
            lax.fori_loop(1, half, lambda hop, carry: (body(hop), carry)[1], 0)

    def slots(owner):
        return pl.ds(pl.multiple_of(owner * width, width), width)

    def block_load(owner):
        return pltpu.make_async_copy(geno_in.at[:, piece(owner)], geno.at[:, piece(owner)], geno_sem.at[owner])

    def coef_load(owner):
        return pltpu.make_async_copy(coef_in.at[:, piece(owner)], coef.at[:, piece(owner)], coef_sem.at[owner])

    def load(owner):
        coef_load(owner).start()
        block_load(owner).start()

    each(count, load)

    barrier = pltpu.get_barrier_semaphore()

    def greet(step):
        pl.semaphore_signal(barrier, inc=1, device_id={"samp": peer(step + 1)}, device_id_type=MESH)

    each(count - 1, greet)
    pl.semaphore_signal(barrier, inc=1, device_id={"var": 1 - var}, device_id_type=MESH)

    def remote(source, target, ssem, rsem, owner):
        return pltpu.make_async_remote_copy(
            src_ref=source, dst_ref=target, send_sem=ssem, recv_sem=rsem,
            device_id={"samp": owner}, device_id_type=MESH,
        )

    def scatter(source, target, ssem, rsem):
        def push(step):
            owner = peer(step + 1)
            remote(source.at[owner], target.at[me], ssem, rsem, owner).start()
        each(count - 1, push)

    def all_in(target, rsem):
        most = target.at[pl.ds(0, count - 1)]
        remote(most, most, rsem, rsem, me + side).wait_recv()

    def arrive(target, rsem, owner):
        remote(target.at[owner], target.at[owner], rsem.at[owner], rsem.at[owner], owner).wait_recv()

    def scattered(source, ssem):
        most = source.at[pl.ds(0, count - 1)]
        remote(most, most, ssem, ssem, me + side).wait_send()

    def swap_with(source, target, ssem, rsem):
        return pltpu.make_async_remote_copy(
            src_ref=source, dst_ref=target, send_sem=ssem, recv_sem=rsem,
            device_id={"var": 1 - var}, device_id_type=MESH,
        )

    fact = facts[...].reshape(1, rows + 2 * columns)
    code = fact[:, :rows].astype(jnp.int32)
    ids_row = (code // CODES).astype(F32)
    down_ranks = lax.broadcasted_iota(jnp.int32, (rows, rows), 0)
    along_ranks = lax.broadcasted_iota(jnp.int32, (rows, rows), 1)
    ids = jnp.sum(jnp.where(down_ranks == along_ranks, ids_row, 0.0), axis=1, keepdims=True)
    owner_row = jnp.floor((ids_row + 0.5) * (1.0 / rows))
    owner_of = jnp.floor((ids + 0.5) * (1.0 / rows))
    before = jnp.sum(
        jnp.where((owner_row == owner_of) & (along_ranks < down_ranks), 1.0, 0.0), axis=1, keepdims=True
    )
    key = (owner_of * width + before).astype(jnp.int32)
    place = (ids - owner_of * rows).astype(jnp.int32)
    ranks = lax.broadcasted_iota(jnp.int32, (rows, width), 0)
    lane = lax.broadcasted_iota(jnp.int32, (rows, width), 1)
    for owner in range(count):
        match = key == lane + owner * width
        place_out[owner] = jnp.max(jnp.where(match, place, -1), axis=0, keepdims=True)
        spot[owner] = jnp.max(jnp.where(match, ranks, -1), axis=0, keepdims=True)

    line = lax.broadcasted_iota(jnp.int32, (8, rows), 0)
    labels = jnp.where(line == 0, code % CODES // 2, jnp.where(line == 1, code % 2, 0)).astype(F32)
    column = lax.broadcasted_iota(jnp.int32, (columns, 2 * columns), 0)
    number = lax.broadcasted_iota(jnp.int32, (columns, 2 * columns), 1)
    rates = fact[:, rows:]
    step_size = jnp.sum(jnp.where(number == column, rates, 0.0), axis=1, keepdims=True)
    least = step_size * jnp.sum(jnp.where(number == column + columns, rates, 0.0), axis=1, keepdims=True)
    column_fold = lax.rem(lax.broadcasted_iota(jnp.int32, (columns, rows), 0), FOLDS).astype(F32)
    trained = jnp.where(labels[0:1, :] != column_fold, 1.0, 0.0)
    counted = trained * labels[1:2, :]
    for group in range(2):
        span = slice(group * few, (group + 1) * few)
        pace[group] = step_size[span]
        threshold[group] = least[span]
        mask[group] = trained[span]
        kept[group] = counted[span]
    place_in[me] = place_out[me]

    pl.semaphore_wait(barrier, count)
    scatter(place_out, place_in, p_ss, p_rs)

    def time_block():
        block = jnp.zeros((rows, width), jnp.int32)
        for owner in range(1, count):
            block += jnp.where(place_in[owner] == ranks, owner, 0)
        return jnp.broadcast_to(jnp.sum(block, axis=1, keepdims=True), (rows, width))

    def return_map():
        block = time_block()
        for owner in range(count):
            span = slice(owner * width, (owner + 1) * width)
            hit = place_in[owner] == ranks
            to_id[:, span] = jnp.where(hit | ((lane == share) & (block > owner)), 1.0, 0.0).astype(BF16)

    def arrange():
        all_in(place_in, p_rs)
        scattered(place_out, p_ss)
        in_totals = (lane - share) == time_block()
        for owner in range(count):
            span = slice(owner * width, (owner + 1) * width)
            hit = place_in[owner] == ranks
            to_time[:, span] = jnp.where(hit | in_totals, 1.0, 0.0).astype(BF16)
        spread = jnp.dot(labels.astype(BF16), to_time[...], preferred_element_type=F32)
        for owner in range(count):
            code_out[owner] = spread[:, owner * width:(owner + 1) * width]
        scatter(code_out, code_in, l_ss, l_rs)
        code_in[me] = code_out[me]

    def sums():
        place_line = lax.broadcasted_iota(jnp.int32, (1, width), 1)
        for owner in range(count):
            span = slice(owner * width, (owner + 1) * width)
            beyond = (place_line >= share + me + 1) & (place_line < share + count)
            reach = jnp.where(beyond, rows, spot[owner])
            back = jnp.where(place_line == share, rows, spot[owner])
            later[:, span] = jnp.where(reach >= ranks, 1.0, 0.0).astype(BF16)
            earlier[:, span] = jnp.where(back >= ranks, 1.0, 0.0).astype(BF16)

    def time_labels():
        all_in(code_in, l_rs)
        scattered(code_out, l_ss)
        labels_time = jnp.zeros((labels.shape[0], rows), F32)
        for owner in range(count):
            labels_time += across(
                code_in[owner].astype(BF16), jnp.where(spot[owner] == ranks, 1.0, 0.0).astype(BF16)
            )
        counted_time = jnp.where(labels_time[0:1, :] != column_fold, 1.0, 0.0) * labels_time[1:2, :]
        for group in range(2):
            kept_time[group] = counted_time[group * few:(group + 1) * few]

    def tell(held_in, hop, band, group):
        block = held_in.at[group, :, piece(me)]
        owner = me + side if hop is None else down(hop)
        index = (0 if hop is None else hop, band)
        return remote(block, block, c_ss, c_rs.at[index], owner)

    def relay(held_in, end, hop, band, group):
        span = piece(up(hop))
        return remote(
            held_in.at[group, :, span], end.at[group, :, span], fwd_ss, fwd_rs.at[hop, band], me + side
        )

    def tell_all(held_in, band, group):
        hops(lambda hop: tell(held_in, hop, band, group).start())
        tell(held_in, None, band, group).start()

    def pass_on(held_in, end, band, group):
        def go(hop):
            tell(held_in, hop, band, group).wait_recv()
            relay(held_in, end, hop, band, group).start()
        hops(go)

    def told():
        sent = low.at[:, :, pl.ds(0, half * part)]
        remote(sent, sent, c_ss, c_ss, me + side).wait_send()
        sent = low.at[:, :, pl.ds(0, (half - 1) * part)]
        remote(sent, sent, fwd_ss, fwd_ss, me + side).wait_send()

    upper = jnp.where(2 * me >= count, 1, 0)

    def far(step):
        return lax.rem(me + jnp.where(upper == 1, step + 1, count - 1 - step), count)

    def spread_far(value, matrix, source, target, ssem, rsem):
        split = halves(value)
        near = upper * half

        def block(first):
            span = pl.ds(pl.multiple_of(first * width, width), half * width)
            both = jnp.dot(split, matrix[:, span], preferred_element_type=F32)
            block = both[:few] + both[few:]
            for owner in range(half):
                source[first + owner] = block[:, owner * width:(owner + 1) * width]

        def push(owner):
            remote(source.at[owner], target.at[me], ssem, rsem.at[me], owner).start()

        block(half - near)
        each(half, lambda step: push(lax.rem(half - near + lax.rem(me + step, half), count)))
        block(near)
        each(half - 1, lambda step: push(near + lax.rem(me + step + 1, half)))

    def gather_far(source, target, rsem, matrix):
        total = across2(source[me], matrix[:, slots(me)])
        for step in range(count - 1):
            owner = far(count - 2 - step)
            arrive(target, rsem, owner)
            total += across2(target[owner], matrix[:, slots(owner)])
        return total

    def send_y(hop, band):
        return remote(out_y.at[hop, band], in_y.at[hop, band], y_ss, y_rs.at[hop, band], me + side)

    def send_z(hop, band):
        return remote(out_z.at[hop, band], in_z.at[hop, band], z_ss, z_rs.at[hop, band], down(hop))

    def add_part(owner, group):
        pred[group] += across(low[group, :, piece(owner)], geno[:, piece(owner)])

    def both_parts(owner):
        both = across(low[:, :, piece(owner)].reshape(columns, part), geno[:, piece(owner)])
        return both.reshape(2, few, rows)

    def one_step(turn, first):
        own = lax.rem(var + turn, 2)
        other = 1 - own
        slot = lax.rem(turn, 2)
        swap = swap_with(pred.at[other], half_recv.at[slot], half_ss, half_rs.at[slot])
        if first:
            pred[...] = jnp.zeros_like(pred)

            def add_block(owner):
                coef_load(owner).wait()
                for group in range(2):
                    low[group, :, piece(owner)] = coef[group * few:(group + 1) * few, piece(owner)].astype(BF16)
                block_load(owner).wait()
                pred[...] += both_parts(owner)
            each(count, add_block)
            swap.start()
            for group in range(2):
                shard[group] = coef[group * few:(group + 1) * few, piece(me)]
            arrange()
        else:
            def add_side(band, group):
                def go(hop):
                    relay(low, low, hop, band, group).wait_recv()
                    add_part(up(hop) + side, group)
                hops(go)

            pred[...] = both_parts(me)
            pass_on(low, low, 0, other)
            tell(low, None, 0, other).wait_recv()
            tell(low, None, 1, own).wait_recv()
            pred[...] += both_parts(me + side)
            pass_on(low, low, 1, own)

            def add_up(hop):
                pred[...] += both_parts(up(hop))
            hops(add_up)
            add_side(0, other)
            swap.start()
            add_side(1, own)
            told()
        swap.wait()

        weight = mask[own] * jnp.exp((pred[own] + half_recv[slot]) * scale_vars)
        held[...] = weight
        spread_far(weight, to_time, out_a, in_a, a_ss, a_rs)
        if first:
            sums()
            time_labels()
        total = gather_far(out_a, in_a, a_rs, later)
        events = kept_time[own]
        ratio = events / jnp.where(events > 0, total, 1.0)
        spread_far(ratio, earlier, out_b, in_b, b_ss, b_rs)
        if first:
            return_map()
        total = gather_far(out_b, in_b, b_rs, to_id)
        score[own] = (held[...] * total - kept[own]).astype(BF16)
        trade = swap_with(score.at[own], score.at[own], s_ss, s_rs)
        trade.start()

        def product(left, owner):
            return jnp.dot(left, geno[:, piece(owner)], preferred_element_type=F32)

        def give(band, group):
            def go(hop):
                out_y[hop, band] = product(score[group], down(hop) + side).astype(BF16)
                send_y(hop, band).start()
            hops(go, (2, 1, 3) if band == 0 else (1, 3, 2))

        def keep(group):
            def go(hop):
                own_g[hop, group] = product(score[group], down(hop))
            hops(go)

        def pairs(band, group):
            def go(hop):
                send_y(hop, band).wait_recv()
                out_z[hop, band] = (own_g[hop, group] + in_y[hop, band].astype(F32)).astype(BF16)
                send_z(hop, band).start()
            hops(go, (2, 1, 3) if band == 0 else (1, 3, 2))

        give(0, own)
        keep(own)
        trade.wait()
        give(1, other)
        pairs(0, own)
        out_y[0] = product(score[...].reshape(columns, rows), me + side).reshape(2, few, part).astype(BF16)
        send_y(0, own).start()
        send_y(0, other).start()
        keep(other)
        pairs(1, other)
        own_g[0] = product(score[...].reshape(columns, rows), me).reshape(2, few, part)

        def update(band, group):
            total = own_g.at[0, group]
            send_y(0, group).wait_recv()
            total[...] += in_y[0, group].astype(F32)

            def go(hop):
                send_z(hop, band).wait_recv()
                total[...] += in_z[hop, band].astype(F32)
            hops(go)
            stepped = shard[group] - pace[group] * (total[...] * scale_samples)
            shrunk = jnp.maximum(jnp.abs(stepped) - threshold[group], 0.0)
            fresh = jnp.where(stepped > 0, shrunk, -shrunk)
            shard[group] = fresh

            def spread_low():
                low[group, :, piece(me)] = fresh.astype(BF16)
                tell_all(low, band, group)

            def spread_change():
                change[group, :, piece(me)] = (fresh - low[group, :, piece(me)].astype(F32)).astype(BF16)
                tell_all(change, band, group)

            if first:
                spread_low()
            else:
                pl.when(turn < ITERS - 1)(spread_low)
                pl.when(turn == ITERS - 1)(spread_change)

        update(0, own)
        update(1, other)
        scattered(out_a, a_ss)
        scattered(out_b, b_ss)
        remote(out_y, out_y, y_ss, y_ss, me + side).wait_send()
        most = out_z.at[pl.ds(1, half - 1)]
        remote(most, most, z_ss, z_ss, me + side).wait_send()

    one_step(0, True)
    lax.fori_loop(1, ITERS, lambda turn, carry: (one_step(turn, False), carry)[1], 0)

    def keep_change(owner):
        span = piece(owner)
        pltpu.make_async_copy(change.at[:, :, span], change_out.at[:, :, span], end_sem.at[2]).start()

    own = lax.rem(var + ITERS - 1, 2)
    keep_change(me)
    low_keep = pltpu.make_async_copy(low, low_out, end_sem.at[0])
    low_keep.start()
    score_wide[...] = score[...].astype(F32)
    score_keep = pltpu.make_async_copy(score_wide, score_out, end_sem.at[1])
    score_keep.start()
    pass_on(change, change_out, 0, own)
    pass_on(change, change_out, 1, 1 - own)
    hops(lambda hop: keep_change(up(hop)))
    tell(change, None, 0, own).wait_recv()
    tell(change, None, 1, 1 - own).wait_recv()
    keep_change(me + side)
    told()
    low_keep.wait()
    score_keep.wait()
    kept_change = pl.ds(0, (half + 1) * part)
    pltpu.make_async_copy(change.at[:, :, kept_change], change_out.at[:, :, kept_change], end_sem.at[2]).wait()
    hops(lambda hop: relay(change, change_out, hop, 0, own).wait_recv())
    hops(lambda hop: relay(change, change_out, hop, 1, 1 - own).wait_recv())


def local(genotypes, coefficients, time_order, fold_label, event_flag, penalty, step_size):
    rows = genotypes.shape[0]
    columns, variants = coefficients.shape
    count = lax.axis_size("samp")
    half = count // 2
    share = rows // count
    width = -(-(share + count) // 128) * 128
    total = count * width
    part = variants // count
    few = columns // 2

    codes = time_order * CODES + fold_label * 2 + event_flag
    facts = jnp.concatenate([codes.astype(F32), step_size, penalty])
    vmem = pl.BlockSpec(memory_space=pltpu.VMEM)
    away = pl.BlockSpec(memory_space=pl.ANY)
    hbm = pl.BlockSpec(memory_space=pltpu.HBM)
    dma = pltpu.SemaphoreType.DMA
    low, change, score = pl.pallas_call(
        functools.partial(path_kernel, count, 1.0 / math.sqrt(VARS), 1.0 / math.sqrt(rows * count)),
        out_shape=(
            jax.ShapeDtypeStruct((2, few, variants), BF16),
            jax.ShapeDtypeStruct((2, few, variants), BF16),
            jax.ShapeDtypeStruct((2, few, rows), F32),
        ),
        in_specs=[hbm] * 2 + [vmem],
        out_specs=(away, away, away),
        scratch_shapes=[
            pltpu.VMEM((rows, variants), BF16),
            pltpu.VMEM((columns, variants), F32),
            pltpu.VMEM((rows, total), BF16),
            pltpu.VMEM((rows, total), BF16),
            pltpu.VMEM((rows, total), BF16),
            pltpu.VMEM((rows, total), BF16),
            pltpu.VMEM((2, few, rows), F32),
            pltpu.VMEM((2, few, rows), F32),
            pltpu.VMEM((2, few, rows), F32),
            pltpu.VMEM((count, 1, width), jnp.int32),
            pltpu.VMEM((count, 1, width), jnp.int32),
            pltpu.VMEM((count, 1, width), jnp.int32),
            pltpu.VMEM((count, 8, width), F32),
            pltpu.VMEM((count, 8, width), F32),
            pltpu.VMEM((2, few, variants), BF16),
            pltpu.VMEM((2, few, variants), BF16),
            pltpu.VMEM((2, few, part), F32),
            pltpu.VMEM((2, few, 1), F32),
            pltpu.VMEM((2, few, 1), F32),
            pltpu.VMEM((2, few, rows), F32),
            pltpu.VMEM((count, few, width), F32),
            pltpu.VMEM((count, few, width), F32),
            pltpu.VMEM((count, few, width), F32),
            pltpu.VMEM((count, few, width), F32),
            pltpu.VMEM((half, 2, few, part), BF16),
            pltpu.VMEM((half, 2, few, part), BF16),
            pltpu.VMEM((half, 2, few, part), BF16),
            pltpu.VMEM((half, 2, few, part), BF16),
            pltpu.VMEM((half, 2, few, part), F32),
            pltpu.VMEM((2, few, rows), F32),
            pltpu.VMEM((few, rows), F32),
            pltpu.VMEM((2, few, rows), BF16),
            pltpu.VMEM((2, few, rows), F32),
            dma((count,)), dma((count,)), dma((3,)),
            dma, dma, dma, dma((2,)),
        ] + [dma] * 10 + [dma((count,))] * 2 + [dma((half, 2))] * 4,
        compiler_params=pltpu.CompilerParams(
            collective_id=0, has_side_effects=True, vmem_limit_bytes=52 * 1024 * 1024
        ),
    )(genotypes, coefficients, facts)
    coefs = low.astype(F32) + change.astype(F32)
    return coefs.reshape(columns, variants), score.astype(BF16).reshape(columns, rows)


def solution(mesh):
    placed = (
        P("samp", "var"),
        P("pheno", "var"),
        P(("pheno", "samp")),
        P(("pheno", "samp")),
        P(("pheno", "samp")),
        P(),
        P(),
    )
    return jax.shard_map(
        local,
        mesh=mesh,
        in_specs=placed,
        out_specs=(P("pheno", "var"), P("pheno", "samp")),
        check_vma=False,
    )
```

```python
import functools
import math

import jax
import jax.numpy as jnp
from jax import lax
from jax.experimental import pallas as pl
from jax.experimental.pallas import tpu as pltpu
from jax.sharding import PartitionSpec as P

VARS = 16384
FOLDS = 8
CODES = 2 * FOLDS
ITERS = 3
MESH = pl.DeviceIdType.MESH
F32 = jnp.float32
BF16 = jnp.bfloat16


def each(count, body):
    if count <= 8:
        for step in range(count):
            body(step)
    else:
        lax.fori_loop(0, count, lambda step, carry: (body(step), carry)[1], 0)


def halves(value):
    high = value.astype(BF16)
    low = (value - high.astype(F32)).astype(BF16)
    return jnp.concatenate([high, low], axis=0)


def across(left, right):
    return lax.dot_general(left, right, (((1,), (1,)), ((), ())), preferred_element_type=F32)


def across2(value, matrix):
    rows = value.shape[0]
    both = across(halves(value), matrix)
    return both[:rows] + both[rows:]


def dot2(value, matrix):
    rows = value.shape[0]
    both = jnp.dot(halves(value), matrix, preferred_element_type=F32)
    return both[:rows] + both[rows:]


def path_kernel(
    count, scale_vars, scale_samples,
    geno_in, coef_in, facts,
    low_out, change_out, score_out,
    geno, coef, to_time, later, earlier, to_id, mask, kept, kept_time, place_out, place_in, spot, code_out, code_in,
    low, change, shard, pace, threshold, half_recv, out_a, in_a, out_b, in_b,
    out_y, in_y, out_z, in_z, own_g, pred, held, score, score_wide,
    geno_sem, coef_sem, end_sem, s_ss, s_rs, half_ss, half_rs, p_ss, l_ss, a_ss, b_ss, y_ss, z_ss, c_ss, fwd_ss,
    p_rs, l_rs, a_rs, b_rs, y_rs, z_rs, c_rs, fwd_rs,
):
    me = lax.axis_index("samp")
    var = lax.axis_index("var")
    columns, variants = coef.shape
    rows = geno.shape[0]
    part = variants // count
    width = later.shape[1] // count
    share = rows // count
    half = count // 2
    few = columns // 2
    side = 1 - 2 * lax.rem(me, 2)

    def peer(step):
        return lax.rem(me + step, count)

    def down(hop):
        return lax.rem(me + 2 * hop, count)

    def up(hop):
        return lax.rem(me + count - 2 * hop, count)

    def piece(owner):
        return pl.ds(pl.multiple_of(owner * part, part), part)

    def hops(body, order=(2, 1, 3)):
        if half <= 8:
            for hop in (order if half == 4 else range(1, half)):
                body(hop)
        else:
            lax.fori_loop(1, half, lambda hop, carry: (body(hop), carry)[1], 0)

    def slots(owner):
        return pl.ds(pl.multiple_of(owner * width, width), width)

    def block_load(owner):
        return pltpu.make_async_copy(geno_in.at[:, piece(owner)], geno.at[:, piece(owner)], geno_sem.at[owner])

    def coef_load(owner):
        return pltpu.make_async_copy(coef_in.at[:, piece(owner)], coef.at[:, piece(owner)], coef_sem.at[owner])

    def load(owner):
        coef_load(owner).start()
        block_load(owner).start()

    each(count, load)

    barrier = pltpu.get_barrier_semaphore()

    def greet(step):
        pl.semaphore_signal(barrier, inc=1, device_id={"samp": peer(step + 1)}, device_id_type=MESH)

    each(count - 1, greet)
    pl.semaphore_signal(barrier, inc=1, device_id={"var": 1 - var}, device_id_type=MESH)

    def remote(source, target, ssem, rsem, owner):
        return pltpu.make_async_remote_copy(
            src_ref=source, dst_ref=target, send_sem=ssem, recv_sem=rsem,
            device_id={"samp": owner}, device_id_type=MESH,
        )

    def scatter(source, target, ssem, rsem):
        def push(step):
            owner = peer(step + 1)
            remote(source.at[owner], target.at[me], ssem, rsem, owner).start()
        each(count - 1, push)

    def all_in(target, rsem):
        most = target.at[pl.ds(0, count - 1)]
        remote(most, most, rsem, rsem, me + side).wait_recv()

    def arrive(target, rsem, owner):
        remote(target.at[owner], target.at[owner], rsem.at[owner], rsem.at[owner], owner).wait_recv()

    def scattered(source, ssem):
        most = source.at[pl.ds(0, count - 1)]
        remote(most, most, ssem, ssem, me + side).wait_send()

    def swap_with(source, target, ssem, rsem):
        return pltpu.make_async_remote_copy(
            src_ref=source, dst_ref=target, send_sem=ssem, recv_sem=rsem,
            device_id={"var": 1 - var}, device_id_type=MESH,
        )

    fact = facts[...].reshape(1, rows + 2 * columns)
    code = fact[:, :rows].astype(jnp.int32)
    ids_row = (code // CODES).astype(F32)
    down_ranks = lax.broadcasted_iota(jnp.int32, (rows, rows), 0)
    along_ranks = lax.broadcasted_iota(jnp.int32, (rows, rows), 1)
    ids = jnp.sum(jnp.where(down_ranks == along_ranks, ids_row, 0.0), axis=1, keepdims=True)
    owner_row = jnp.floor((ids_row + 0.5) * (1.0 / rows))
    owner_of = jnp.floor((ids + 0.5) * (1.0 / rows))
    before = jnp.sum(
        jnp.where((owner_row == owner_of) & (along_ranks < down_ranks), 1.0, 0.0), axis=1, keepdims=True
    )
    key = (owner_of * width + before).astype(jnp.int32)
    place = (ids - owner_of * rows).astype(jnp.int32)
    ranks = lax.broadcasted_iota(jnp.int32, (rows, width), 0)
    lane = lax.broadcasted_iota(jnp.int32, (rows, width), 1)
    for owner in range(count):
        match = key == lane + owner * width
        place_out[owner] = jnp.max(jnp.where(match, place, -1), axis=0, keepdims=True)
        spot[owner] = jnp.max(jnp.where(match, ranks, -1), axis=0, keepdims=True)

    line = lax.broadcasted_iota(jnp.int32, (8, rows), 0)
    labels = jnp.where(line == 0, code % CODES // 2, jnp.where(line == 1, code % 2, 0)).astype(F32)
    column = lax.broadcasted_iota(jnp.int32, (columns, 2 * columns), 0)
    number = lax.broadcasted_iota(jnp.int32, (columns, 2 * columns), 1)
    rates = fact[:, rows:]
    step_size = jnp.sum(jnp.where(number == column, rates, 0.0), axis=1, keepdims=True)
    least = step_size * jnp.sum(jnp.where(number == column + columns, rates, 0.0), axis=1, keepdims=True)
    column_fold = lax.rem(lax.broadcasted_iota(jnp.int32, (columns, rows), 0), FOLDS).astype(F32)
    trained = jnp.where(labels[0:1, :] != column_fold, 1.0, 0.0)
    counted = trained * labels[1:2, :]
    for group in range(2):
        span = slice(group * few, (group + 1) * few)
        pace[group] = step_size[span]
        threshold[group] = least[span]
        mask[group] = trained[span]
        kept[group] = counted[span]
    place_in[me] = place_out[me]

    pl.semaphore_wait(barrier, count)
    scatter(place_out, place_in, p_ss, p_rs)

    def time_block():
        block = jnp.zeros((rows, width), jnp.int32)
        for owner in range(1, count):
            block += jnp.where(place_in[owner] == ranks, owner, 0)
        return jnp.broadcast_to(jnp.sum(block, axis=1, keepdims=True), (rows, width))

    def return_map():
        block = time_block()
        for owner in range(count):
            span = slice(owner * width, (owner + 1) * width)
            hit = place_in[owner] == ranks
            to_id[:, span] = jnp.where(hit | ((lane == share) & (block > owner)), 1.0, 0.0).astype(BF16)

    def arrange():
        all_in(place_in, p_rs)
        scattered(place_out, p_ss)
        in_totals = (lane - share) == time_block()
        for owner in range(count):
            span = slice(owner * width, (owner + 1) * width)
            hit = place_in[owner] == ranks
            to_time[:, span] = jnp.where(hit | in_totals, 1.0, 0.0).astype(BF16)
        spread = jnp.dot(labels.astype(BF16), to_time[...], preferred_element_type=F32)
        for owner in range(count):
            code_out[owner] = spread[:, owner * width:(owner + 1) * width]
        scatter(code_out, code_in, l_ss, l_rs)
        code_in[me] = code_out[me]

    def sums():
        place_line = lax.broadcasted_iota(jnp.int32, (1, width), 1)
        for owner in range(count):
            span = slice(owner * width, (owner + 1) * width)
            beyond = (place_line >= share + me + 1) & (place_line < share + count)
            reach = jnp.where(beyond, rows, spot[owner])
            back = jnp.where(place_line == share, rows, spot[owner])
            later[:, span] = jnp.where(reach >= ranks, 1.0, 0.0).astype(BF16)
            earlier[:, span] = jnp.where(back >= ranks, 1.0, 0.0).astype(BF16)

    def time_labels():
        all_in(code_in, l_rs)
        scattered(code_out, l_ss)
        labels_time = jnp.zeros((labels.shape[0], rows), F32)
        for owner in range(count):
            labels_time += across(
                code_in[owner].astype(BF16), jnp.where(spot[owner] == ranks, 1.0, 0.0).astype(BF16)
            )
        counted_time = jnp.where(labels_time[0:1, :] != column_fold, 1.0, 0.0) * labels_time[1:2, :]
        for group in range(2):
            kept_time[group] = counted_time[group * few:(group + 1) * few]

    def tell(held_in, hop, band, group):
        block = held_in.at[group, :, piece(me)]
        owner = me + side if hop is None else down(hop)
        index = (0 if hop is None else hop, band)
        return remote(block, block, c_ss, c_rs.at[index], owner)

    def relay(held_in, end, hop, band, group):
        span = piece(up(hop))
        return remote(
            held_in.at[group, :, span], end.at[group, :, span], fwd_ss, fwd_rs.at[hop, band], me + side
        )

    def tell_all(held_in, band, group):
        hops(lambda hop: tell(held_in, hop, band, group).start())
        tell(held_in, None, band, group).start()

    def pass_on(held_in, end, band, group):
        def go(hop):
            tell(held_in, hop, band, group).wait_recv()
            relay(held_in, end, hop, band, group).start()
        hops(go)

    def told():
        sent = low.at[:, :, pl.ds(0, half * part)]
        remote(sent, sent, c_ss, c_ss, me + side).wait_send()
        sent = low.at[:, :, pl.ds(0, (half - 1) * part)]
        remote(sent, sent, fwd_ss, fwd_ss, me + side).wait_send()

    upper = jnp.where(2 * me >= count, 1, 0)

    def far(step):
        return lax.rem(me + jnp.where(upper == 1, step + 1, count - 1 - step), count)

    def spread_far(value, matrix, source, target, ssem, rsem):
        split = halves(value)
        near = upper * half

        def block(first):
            span = pl.ds(pl.multiple_of(first * width, width), half * width)
            both = jnp.dot(split, matrix[:, span], preferred_element_type=F32)
            block = both[:few] + both[few:]
            for owner in range(half):
                source[first + owner] = block[:, owner * width:(owner + 1) * width]

        def push(owner):
            remote(source.at[owner], target.at[me], ssem, rsem.at[me], owner).start()

        block(half - near)
        each(half, lambda step: push(lax.rem(half - near + lax.rem(me + step, half), count)))
        block(near)
        each(half - 1, lambda step: push(near + lax.rem(me + step + 1, half)))

    def gather_far(source, target, rsem, matrix):
        total = across2(source[me], matrix[:, slots(me)])
        for step in range(count - 1):
            owner = far(count - 2 - step)
            arrive(target, rsem, owner)
            total += across2(target[owner], matrix[:, slots(owner)])
        return total

    def send_y(hop, band):
        return remote(out_y.at[hop, band], in_y.at[hop, band], y_ss, y_rs.at[hop, band], me + side)

    def send_z(hop, band):
        return remote(out_z.at[hop, band], in_z.at[hop, band], z_ss, z_rs.at[hop, band], down(hop))

    def add_part(owner, group):
        pred[group] += across(low[group, :, piece(owner)], geno[:, piece(owner)])

    def both_parts(owner):
        both = across(low[:, :, piece(owner)].reshape(columns, part), geno[:, piece(owner)])
        return both.reshape(2, few, rows)

    def one_step(turn, first):
        own = lax.rem(var + turn, 2)
        other = 1 - own
        slot = lax.rem(turn, 2)
        swap = swap_with(pred.at[other], half_recv.at[slot], half_ss, half_rs.at[slot])
        if first:
            pred[...] = jnp.zeros_like(pred)

            def add_block(owner):
                coef_load(owner).wait()
                for group in range(2):
                    low[group, :, piece(owner)] = coef[group * few:(group + 1) * few, piece(owner)].astype(BF16)
                block_load(owner).wait()
                pred[...] += both_parts(owner)
            each(count, add_block)
            swap.start()
            for group in range(2):
                shard[group] = coef[group * few:(group + 1) * few, piece(me)]
            arrange()
        else:
            def add_side(band, group):
                def go(hop):
                    relay(low, low, hop, band, group).wait_recv()
                    add_part(up(hop) + side, group)
                hops(go)

            pred[...] = both_parts(me)
            pass_on(low, low, 0, other)
            tell(low, None, 0, other).wait_recv()
            tell(low, None, 1, own).wait_recv()
            pred[...] += both_parts(me + side)
            pass_on(low, low, 1, own)

            def add_up(hop):
                pred[...] += both_parts(up(hop))
            hops(add_up)
            add_side(0, other)
            swap.start()
            add_side(1, own)
            told()
        swap.wait()

        weight = mask[own] * jnp.exp((pred[own] + half_recv[slot]) * scale_vars)
        held[...] = weight
        spread_far(weight, to_time, out_a, in_a, a_ss, a_rs)
        if first:
            sums()
            time_labels()
        total = gather_far(out_a, in_a, a_rs, later)
        events = kept_time[own]
        ratio = events / jnp.where(events > 0, total, 1.0)
        spread_far(ratio, earlier, out_b, in_b, b_ss, b_rs)
        if first:
            return_map()
        total = gather_far(out_b, in_b, b_rs, to_id)
        score[own] = (held[...] * total - kept[own]).astype(BF16)
        trade = swap_with(score.at[own], score.at[own], s_ss, s_rs)
        trade.start()

        def product(left, owner):
            return jnp.dot(left, geno[:, piece(owner)], preferred_element_type=F32)

        def give(band, group):
            def go(hop):
                out_y[hop, band] = product(score[group], down(hop) + side).astype(BF16)
                send_y(hop, band).start()
            hops(go, (2, 1, 3) if band == 0 else (1, 3, 2))

        def keep(group):
            def go(hop):
                own_g[hop, group] = product(score[group], down(hop))
            hops(go)

        def pairs(band, group):
            def go(hop):
                send_y(hop, band).wait_recv()
                out_z[hop, band] = (own_g[hop, group] + in_y[hop, band].astype(F32)).astype(BF16)
                send_z(hop, band).start()
            hops(go, (2, 1, 3) if band == 0 else (1, 3, 2))

        give(0, own)
        keep(own)
        trade.wait()
        give(1, other)
        pairs(0, own)
        keep(other)
        out_y[0] = product(score[...].reshape(columns, rows), me + side).reshape(2, few, part).astype(BF16)
        send_y(0, own).start()
        send_y(0, other).start()
        pairs(1, other)
        own_g[0] = product(score[...].reshape(columns, rows), me).reshape(2, few, part)

        def update(band, group):
            total = own_g.at[0, group]
            send_y(0, group).wait_recv()
            total[...] += in_y[0, group].astype(F32)

            def go(hop):
                send_z(hop, band).wait_recv()
                total[...] += in_z[hop, band].astype(F32)
            hops(go)
            stepped = shard[group] - pace[group] * (total[...] * scale_samples)
            shrunk = jnp.maximum(jnp.abs(stepped) - threshold[group], 0.0)
            fresh = jnp.where(stepped > 0, shrunk, -shrunk)
            shard[group] = fresh

            def spread_low():
                low[group, :, piece(me)] = fresh.astype(BF16)
                tell_all(low, band, group)

            def spread_change():
                change[group, :, piece(me)] = (fresh - low[group, :, piece(me)].astype(F32)).astype(BF16)
                tell_all(change, band, group)

            if first:
                spread_low()
            else:
                pl.when(turn < ITERS - 1)(spread_low)
                pl.when(turn == ITERS - 1)(spread_change)

        update(0, own)
        update(1, other)
        scattered(out_a, a_ss)
        scattered(out_b, b_ss)
        remote(out_y, out_y, y_ss, y_ss, me + side).wait_send()
        most = out_z.at[pl.ds(1, half - 1)]
        remote(most, most, z_ss, z_ss, me + side).wait_send()

    one_step(0, True)
    lax.fori_loop(1, ITERS, lambda turn, carry: (one_step(turn, False), carry)[1], 0)

    def keep_change(owner):
        span = piece(owner)
        pltpu.make_async_copy(change.at[:, :, span], change_out.at[:, :, span], end_sem.at[2]).start()

    own = lax.rem(var + ITERS - 1, 2)
    keep_change(me)
    low_keep = pltpu.make_async_copy(low, low_out, end_sem.at[0])
    low_keep.start()
    score_wide[...] = score[...].astype(F32)
    score_keep = pltpu.make_async_copy(score_wide, score_out, end_sem.at[1])
    score_keep.start()
    pass_on(change, change_out, 0, own)
    pass_on(change, change_out, 1, 1 - own)
    hops(lambda hop: keep_change(up(hop)))
    tell(change, None, 0, own).wait_recv()
    tell(change, None, 1, 1 - own).wait_recv()
    keep_change(me + side)
    told()
    low_keep.wait()
    score_keep.wait()
    kept_change = pl.ds(0, (half + 1) * part)
    pltpu.make_async_copy(change.at[:, :, kept_change], change_out.at[:, :, kept_change], end_sem.at[2]).wait()
    hops(lambda hop: relay(change, change_out, hop, 0, own).wait_recv())
    hops(lambda hop: relay(change, change_out, hop, 1, 1 - own).wait_recv())


def local(genotypes, coefficients, time_order, fold_label, event_flag, penalty, step_size):
    rows = genotypes.shape[0]
    columns, variants = coefficients.shape
    count = lax.axis_size("samp")
    half = count // 2
    share = rows // count
    width = -(-(share + count) // 128) * 128
    total = count * width
    part = variants // count
    few = columns // 2

    codes = time_order * CODES + fold_label * 2 + event_flag
    facts = jnp.concatenate([codes.astype(F32), step_size, penalty])
    vmem = pl.BlockSpec(memory_space=pltpu.VMEM)
    away = pl.BlockSpec(memory_space=pl.ANY)
    hbm = pl.BlockSpec(memory_space=pltpu.HBM)
    dma = pltpu.SemaphoreType.DMA
    low, change, score = pl.pallas_call(
        functools.partial(path_kernel, count, 1.0 / math.sqrt(VARS), 1.0 / math.sqrt(rows * count)),
        out_shape=(
            jax.ShapeDtypeStruct((2, few, variants), BF16),
            jax.ShapeDtypeStruct((2, few, variants), BF16),
            jax.ShapeDtypeStruct((2, few, rows), F32),
        ),
        in_specs=[hbm] * 2 + [vmem],
        out_specs=(away, away, away),
        scratch_shapes=[
            pltpu.VMEM((rows, variants), BF16),
            pltpu.VMEM((columns, variants), F32),
            pltpu.VMEM((rows, total), BF16),
            pltpu.VMEM((rows, total), BF16),
            pltpu.VMEM((rows, total), BF16),
            pltpu.VMEM((rows, total), BF16),
            pltpu.VMEM((2, few, rows), F32),
            pltpu.VMEM((2, few, rows), F32),
            pltpu.VMEM((2, few, rows), F32),
            pltpu.VMEM((count, 1, width), jnp.int32),
            pltpu.VMEM((count, 1, width), jnp.int32),
            pltpu.VMEM((count, 1, width), jnp.int32),
            pltpu.VMEM((count, 8, width), F32),
            pltpu.VMEM((count, 8, width), F32),
            pltpu.VMEM((2, few, variants), BF16),
            pltpu.VMEM((2, few, variants), BF16),
            pltpu.VMEM((2, few, part), F32),
            pltpu.VMEM((2, few, 1), F32),
            pltpu.VMEM((2, few, 1), F32),
            pltpu.VMEM((2, few, rows), F32),
            pltpu.VMEM((count, few, width), F32),
            pltpu.VMEM((count, few, width), F32),
            pltpu.VMEM((count, few, width), F32),
            pltpu.VMEM((count, few, width), F32),
            pltpu.VMEM((half, 2, few, part), BF16),
            pltpu.VMEM((half, 2, few, part), BF16),
            pltpu.VMEM((half, 2, few, part), BF16),
            pltpu.VMEM((half, 2, few, part), BF16),
            pltpu.VMEM((half, 2, few, part), F32),
            pltpu.VMEM((2, few, rows), F32),
            pltpu.VMEM((few, rows), F32),
            pltpu.VMEM((2, few, rows), BF16),
            pltpu.VMEM((2, few, rows), F32),
            dma((count,)), dma((count,)), dma((3,)),
            dma, dma, dma, dma((2,)),
        ] + [dma] * 10 + [dma((count,))] * 2 + [dma((half, 2))] * 4,
        compiler_params=pltpu.CompilerParams(
            collective_id=0, has_side_effects=True, vmem_limit_bytes=52 * 1024 * 1024
        ),
    )(genotypes, coefficients, facts)
    coefs = low.astype(F32) + change.astype(F32)
    return coefs.reshape(columns, variants), score.astype(BF16).reshape(columns, rows)


def solution(mesh):
    placed = (
        P("samp", "var"),
        P("pheno", "var"),
        P(("pheno", "samp")),
        P(("pheno", "samp")),
        P(("pheno", "samp")),
        P(),
        P(),
    )
    return jax.shard_map(
        local,
        mesh=mesh,
        in_specs=placed,
        out_specs=(P("pheno", "var"), P("pheno", "samp")),
        check_vma=False,
    )
```
